256 devices in a mesh: gx: 16 (over y, z_lo), gy: 16 (over x, z_hi, core).
Axes of the slice: x: 4, y: 4, z: 8 (z_hi: 2, z_lo: 4; z = z_hi * 4 + z_lo), core: 2. Of those that a mesh axis runs over, the one named last changes fastest.
Arguments:
- densities: bfloat16 [16, 16, 64, 8192], P('gx', 'gy'), may hold values from -6 to 6
- trials: bfloat16 [16, 16, 64, 256], P('gx', 'gy'), may hold values from -6 to 6
- energies: float32 [16, 16, 64, 8], P('gx', 'gy'), may hold values from 1 to 4
- metric: bfloat16 [1024, 1024], replicated, may hold values from -0.1875 to 0.1875
- pair_local: int32 [16, 16, 6912], P('gx', 'gy'), may hold values from 0 to 63
- pair_remote: int32 [16, 16, 6912], P('gx', 'gy'), may hold values from 0 to 63, as said below
- pair_scale: float32 [16, 16, 6912], P('gx', 'gy'), may hold values from 0.2 to 2
Outputs:
- sigma_first: float32 [16, 16, 64, 256], P('gx', 'gy')
- corrections: bfloat16 [16, 16, 64, 256], P('gx', 'gy')
- sigma_second: float32 [16, 16, 64, 256], P('gx', 'gy')
- theta: float32 [32], replicated
The draws below stay inside these ranges and needn't reach their ends.
Inputs may be any that keep to these rules, and one draw needn't show every extreme that they name: pair_remote is below 63 in the slots of the bin's own block (p // 768 = 4); in the other slots it takes every value up to 63.
All inputs are finite; a program needn't handle non-finite values.
Results may differ from the reference program's by a relative error of at most 0.0057.
Values may be sent and summed in bfloat16 or wider, within the bound.
No kernel may reach another device: no remote copies, remote signals or barrier semaphores. Data moves between devices by JAX's collectives and lax.ppermute only.
A program may use at most 128 MiB of HBM per device.

```python
import math
import jax
import jax.numpy as jnp
from jax import lax

AUX = 1024
STATES = 8
VECS = 32
MOL_DEV = 64
CAP = 768
PAIRS = 6912
GRID_X = 16
GRID_Y = 16


def draw_pair_remote(key, part):
    owner = jnp.arange(PAIRS, dtype=jnp.int32) // CAP
    upper = jnp.where(owner == 4, MOL_DEV - 1, MOL_DEV).astype(jnp.int32)
    upper = jnp.broadcast_to(upper, (GRID_X, GRID_Y, PAIRS))
    return jax.random.randint(jax.random.fold_in(key, 17), (GRID_X, GRID_Y, PAIRS), 0, upper, dtype=jnp.int32)


def place_ends(result, stream_key, least, largest):
    extent = result.shape
    place = [jax.random.randint(jax.random.fold_in(stream_key, axis), (), 0, extent[axis]) for axis in range(len(extent))]
    result = result.at[tuple(place)].set(least)
    longest = extent.index(max(extent))
    place[longest] = (place[longest] + 1) % extent[longest]
    return result.at[tuple(place)].set(largest)


def level_of(own_key, shape, pieces, low, top_value):
    factor_of = 1.0
    for position, shards_of in pieces:
        steps = jax.random.uniform(jax.random.fold_in(jax.random.fold_in(own_key, 6), position), (shards_of,), jnp.float32, low / len(pieces), top_value / len(pieces))
        factor_of = factor_of * jnp.repeat(jnp.exp(steps), shape[position] // shards_of).reshape((-1,) + (1,) * (len(shape) - 1 - position))
    return factor_of


def noise(key, extent, deviation, most, cuts=(), kind=jnp.bfloat16):
    entries = deviation * jax.random.normal(key, extent, jnp.float32)
    if cuts:
        entries = entries * level_of(key, extent, cuts, -0.22, 0.18)
    return jnp.clip(entries, -most, most).astype(kind)


def setup_inputs(seed: int = 0) -> dict:
    key_list = jax.random.split(jax.random.key(seed), 8)
    return {
        "densities": noise(key_list[0], (GRID_X, GRID_Y, MOL_DEV, STATES * AUX), 1.0, 6.0, ((0, 16), (1, 16))),
        "trials": noise(key_list[1], (GRID_X, GRID_Y, MOL_DEV, STATES * VECS), 1.0, 6.0, ((0, 16), (1, 16))),
        "energies": jnp.clip(jnp.exp(math.log(4.0) - 1.3862944 * jax.random.uniform(key_list[2], (GRID_X, GRID_Y, MOL_DEV, STATES), jnp.float32) ** level_of(key_list[2], (GRID_X, GRID_Y, MOL_DEV, STATES), ((0, 16), (1, 16)), -0.2, 0.2)), 1.0, 4.0),
        "metric": noise(key_list[3], (AUX, AUX), AUX ** -0.5, 0.1875),
        "pair_local": place_ends(jax.random.randint(key_list[4], (GRID_X, GRID_Y, PAIRS), 0, MOL_DEV), jax.random.fold_in(key_list[4], 1), 0, MOL_DEV - 1).astype(jnp.int32),
        "pair_remote": draw_pair_remote(jax.random.fold_in(key_list[7], 71), 0),
        "pair_scale": jnp.clip(jnp.exp(math.log(2.0) - 2.3025851 * jax.random.uniform(key_list[6], (GRID_X, GRID_Y, PAIRS), jnp.float32) ** level_of(key_list[6], (GRID_X, GRID_Y, PAIRS), ((0, 16), (1, 16)), -0.2, 0.2)), 0.2, 2.0),
    }


def partner_index(bin_id, local, remote):
    bx = bin_id // GRID_Y
    by = bin_id % GRID_Y
    owner = jnp.arange(PAIRS, dtype=jnp.int32) // CAP
    nbin = (bx + owner // 3 - 1) % GRID_X * GRID_Y + (by + owner % 3 - 1) % GRID_Y
    inner = jnp.where(owner == 4, (local + 1 + remote) % MOL_DEV, remote)
    return (nbin * MOL_DEV + inner).astype(jnp.int32)

def reference(densities, trials, energies, metric, pair_local, pair_remote, pair_scale):
    nbins = GRID_X * GRID_Y
    flat_rho = densities.reshape(nbins * MOL_DEV, STATES, AUX)
    locals_all = pair_local.reshape(nbins, PAIRS)
    remotes_all = pair_remote.reshape(nbins, PAIRS)
    scales_all = pair_scale.reshape(nbins, PAIRS)
    bin_ids = jnp.arange(nbins, dtype=jnp.int32)
    index_all = jax.vmap(partner_index)(bin_ids, locals_all, remotes_all)
    energy_all = energies.reshape(nbins, MOL_DEV, STATES)

    def couple(items):
        bin_id, local, index, scale = items
        start = (bin_id * MOL_DEV).astype(jnp.int32)
        rho_bin = lax.dynamic_slice_in_dim(flat_rho, start, MOL_DEV, 0)
        proj = jnp.dot(rho_bin.reshape(MOL_DEV * STATES, AUX), metric, preferred_element_type=jnp.float32)
        proj = proj.astype(jnp.bfloat16).reshape(MOL_DEV, STATES, AUX)
        left = proj[local].astype(jnp.float32)
        right = flat_rho[index].astype(jnp.float32)
        block = jnp.einsum('pas,pbs->pab', left, right, precision=lax.Precision.HIGHEST)
        return block * (scale / jnp.sqrt(jnp.float32(AUX)))[:, None, None]
    couplings = lax.map(couple, (bin_ids, locals_all, index_all, scales_all))

    def matvec(field):
        flat = field.reshape(nbins * MOL_DEV, STATES, VECS)

        def one_bin(items):
            block, local, index, energy, own = items
            near = flat[index]
            contrib = jnp.einsum('pab,pbv->pav', block, near, precision=lax.Precision.HIGHEST)
            summed = jax.ops.segment_sum(contrib, local, MOL_DEV)
            return summed + energy[:, :, None] * own
        return lax.map(one_bin, (couplings, locals_all, index_all, energy_all, field))
    start_vecs = trials.astype(jnp.float32).reshape(nbins, MOL_DEV, STATES, VECS)
    sigma_first = matvec(start_vecs)
    numer = lax.optimization_barrier(jnp.sum(start_vecs * sigma_first, axis=(0, 1, 2)))
    denom = lax.optimization_barrier(jnp.sum(start_vecs * start_vecs, axis=(0, 1, 2)))
    theta = numer / denom
    resid = (sigma_first - theta * start_vecs) / jnp.maximum(jnp.abs(energy_all[:, :, :, None] - theta), 1.0)
    mean_sq = lax.optimization_barrier(jnp.sum(resid * resid, axis=(0, 1, 2))) / (nbins * MOL_DEV * STATES)
    corrections = (resid / jnp.sqrt(mean_sq + 1e-06)).astype(jnp.bfloat16)
    sigma_second = matvec(corrections.astype(jnp.float32))
    shape = (GRID_X, GRID_Y, MOL_DEV, STATES * VECS)
    return (sigma_first.reshape(shape), corrections.reshape(shape), sigma_second.reshape(shape), theta)
```

```python
import functools

import jax
import jax.numpy as jnp
from jax import lax
from jax.experimental import pallas as pl
from jax.experimental.pallas import tpu as pltpu
from jax.sharding import PartitionSpec as P

BF = jnp.bfloat16
F32 = jnp.float32
AXES = ("gx", "gy")
SELF, TO_R, TO_U, TO_UR = 4, 7, 5, 8
R_TO_A, R_TO_U, U_TO_A, U_TO_R, UR_TO_A = 1, 2, 3, 6, 0


def vmem(count):
    return [pl.BlockSpec(memory_space=pltpu.VMEM)] * count


def call(body, outs, flops, moved):
    return lambda *args: pl.pallas_call(
        body,
        out_shape=outs,
        in_specs=vmem(len(args)),
        out_specs=jax.tree.map(lambda _: pl.BlockSpec(memory_space=pltpu.VMEM), outs),
        compiler_params=pltpu.CompilerParams(vmem_limit_bytes=60 * 2**20),
        cost_estimate=pl.CostEstimate(flops=flops, bytes_accessed=moved, transcendentals=0),
    )(*args)


def shape(*dims, dtype=F32):
    return jax.ShapeDtypeStruct(dims, dtype)


def stack(ref, states):
    width = ref.shape[1] // states
    return jnp.concatenate([ref[:, a * width : (a + 1) * width] for a in range(states)], axis=0)


def unstack(value, states):
    mols = value.shape[0] // states
    return jnp.concatenate([value[a * mols : (a + 1) * mols] for a in range(states)], axis=1)


def dot_nt(a, b):
    return lax.dot_general(a, b, (((1,), (1,)), ((), ())), preferred_element_type=F32)


def dot(a, b):
    return jnp.dot(a, b, preferred_element_type=F32)


def twice(w):
    return jnp.concatenate([w, w], axis=1)


def couple(proj, rho, pair):
    dense = dot_nt(proj, rho)
    tiles = (dense.shape[0] // pair.shape[0], dense.shape[1] // pair.shape[1])
    return (dense * jnp.tile(pair, tiles)).astype(BF)


def spread(e, width):
    mols, states = e.shape
    lane = lax.broadcasted_iota(jnp.int32, (mols, states * width), 1) // width
    out = jnp.zeros((mols, states * width), F32)
    for a in range(states):
        out = jnp.where(lane == a, e[:, a : a + 1], out)
    return out


def weights_body(scale, loc, rem, sc, y, e, own, msg):
    mols = y.shape[0]
    cap = loc.shape[1] // 9
    mol = lax.broadcasted_iota(jnp.int32, (mols, cap), 0)

    def weight(o):
        part = slice(o * cap, (o + 1) * cap)
        left, right, factor = loc[:, part], rem[:, part], sc[:, part] * scale
        if o == 4:
            right = left + 1 + right
            right = jnp.where(right >= mols, right - mols, right)
        mine = jnp.where(mol == left, factor, 0.0)
        far = jnp.where(mol == right, 1.0, 0.0).astype(BF)
        high = mine.astype(BF)
        rest = mine - high.astype(F32)
        mid = rest.astype(BF)
        low = (rest - mid.astype(F32)).astype(BF)
        three = dot_nt(
            jnp.concatenate([high, mid, low], axis=0), jnp.concatenate([far, far], axis=0)
        )
        return three[:mols] + (three[mols : 2 * mols] + three[2 * mols :])

    for k, o in enumerate((SELF, TO_R, TO_U, TO_UR)):
        own[k] = weight(o)
    field = y.shape[1]
    for k, (o, q) in enumerate(((R_TO_A, R_TO_U), (U_TO_A, U_TO_R), (UR_TO_A, None))):
        first = weight(o)
        if q is not None:
            lane = lax.broadcasted_iota(jnp.int32, first.shape, 1)
            first = jnp.where(lane < mols, first, weight(q))
        msg[k, :, :field] = y[...].astype(F32)
        msg[k, :, field : field + 2 * mols] = first
        msg[k, :, field + 2 * mols :] = jnp.concatenate(
            [e[...], jnp.zeros((mols, 2 * mols - e.shape[1]), F32)], axis=1
        )


def self_body(states, rho, metric, own, proj, c_aa):
    rows = stack(rho, states)
    proj[...] = dot(rows, metric[...]).astype(BF)
    c_aa[...] = couple(proj[...], rows, own[0])


def right_body(states, rho_a, rho_r, metric, proj_a, own, msg_r, proj_r, c):
    mols = rho_a.shape[0]
    rows_a, rows_r = stack(rho_a, states), stack(rho_r, states)
    field = msg_r.shape[1] - 4 * mols
    c[0] = couple(proj_a[...], rows_r, own[1])
    proj_r[...] = dot(rows_r, metric[...]).astype(BF)
    c[1] = couple(proj_r[...], rows_a, twice(msg_r[:, field : field + mols]))


def up_body(
    states, rho_a, rho_r, rho_u, metric, proj_a, proj_r, own, msg_r, msg_u, c_aa, c_r, y_a, c, sig
):
    mols = rho_a.shape[0]
    field = msg_r.shape[1] - 4 * mols
    rows_u = stack(rho_u, states)
    c[0] = couple(proj_a[...], rows_u, own[2])
    c[1] = couple(proj_r[...], rows_u, twice(msg_r[:, field + mols : field + 2 * mols]))
    proj_u = dot(rows_u, metric[...]).astype(BF)
    c[2] = couple(proj_u, stack(rho_a, states), twice(msg_u[:, field : field + mols]))
    c[3] = couple(
        proj_u, stack(rho_r, states), twice(msg_u[:, field + mols : field + 2 * mols])
    )
    f_a = stack(y_a, states)
    f_r = stack(msg_r[:, :field], states).astype(BF)
    f_u = stack(msg_u[:, :field], states).astype(BF)
    sig[0] = dot(c_aa[...], f_a) + (dot(c_r[0], f_r) + dot(c[0], f_u))
    sig[1] = dot(c_r[1], f_a) + dot(c[1], f_u)
    sig[2] = dot(c[2], f_a) + dot(c[3], f_r)


def corner_body(
    states, rho_a, rho_c, metric, proj_a, own, msg_r, msg_u, msg_c, y_a, e_a, sig, c, parts, sums
):
    mols = rho_a.shape[0]
    field = msg_r.shape[1] - 4 * mols
    rows_c = stack(rho_c, states)
    c[0] = couple(proj_a[...], rows_c, own[3])
    proj_c = dot(rows_c, metric[...]).astype(BF)
    c[1] = couple(proj_c, stack(rho_a, states), twice(msg_c[:, field : field + mols]))
    f_a = stack(y_a, states)
    f_c = stack(msg_c[:, :field], states).astype(BF)
    own_y = y_a[...].astype(F32)
    part_a = unstack(sig[0] + dot(c[0], f_c), states)
    part_a = part_a + spread(e_a[...], field // states) * own_y
    part_r = unstack(sig[1], states)
    part_u = unstack(sig[2], states)
    part_c = unstack(dot(c[1], f_a), states)
    parts[0], parts[1], parts[2], parts[3] = part_a, part_r, part_u, part_c
    total = part_a * own_y + part_r * msg_r[:, :field]
    total = total + (part_u * msg_u[:, :field] + part_c * msg_c[:, :field])
    sums[0:1] = jnp.sum(total, axis=0, keepdims=True)
    sums[1:2] = jnp.sum(own_y * own_y, axis=0, keepdims=True)


def over_states(row, width):
    states = row.shape[1] // width
    total = row[:, :width]
    for a in range(1, states):
        total = total + row[:, a * width : (a + 1) * width]
    return jnp.concatenate([total] * states, axis=1)


def residual(sigma, y, e, theta, width):
    return (sigma - theta * y) / jnp.maximum(jnp.abs(spread(e, width) - theta), 1.0)


def theta_body(states, sums, sigma, y_a, e_a, theta, resid, squares):
    width = sigma.shape[1] // states
    rate = over_states(sums[0:1], width) / over_states(sums[1:2], width)
    theta[...] = rate
    value = residual(sigma[...], y_a[...].astype(F32), e_a[...], rate, width)
    resid[...] = value
    squares[...] = jnp.sum(value * value, axis=0, keepdims=True)


def second_body(
    states, theta, resid, sig_r, sig_u, sig_c, msg_r, msg_u, msg_c, c_aa, c_r, c_u, c_c, parts
):
    mols, field = resid.shape
    width = field // states

    def other(sigma, msg):
        e = msg[:, field + 2 * mols : field + 2 * mols + states]
        value = residual(sigma, msg[:, :field], e, theta[...], width)
        return stack(value, states).astype(BF)

    f_a = stack(resid[...], states).astype(BF)
    f_r = other(sig_r[...], msg_r)
    f_u = other(sig_u[...], msg_u)
    f_c = other(sig_c[...], msg_c)
    row_a = (dot(c_aa[...], f_a) + dot(c_r[0], f_r)) + (dot(c_u[0], f_u) + dot(c_c[0], f_c))
    parts[0] = unstack(row_a, states)
    parts[1] = unstack(dot(c_r[1], f_a) + dot(c_u[1], f_u), states)
    parts[2] = unstack(dot(c_u[2], f_a) + dot(c_u[3], f_r), states)
    parts[3] = unstack(dot(c_c[1], f_a), states)


def last_body(states, count, squares, resid, raw, e_a, corr, sigma):
    width = resid.shape[1] // states
    scale = jnp.sqrt(over_states(squares[...], width) / count + 1e-06)
    value = (resid[...] / scale).astype(BF)
    corr[...] = value
    sigma[...] = raw[...] / scale + spread(e_a[...], width) * value.astype(F32)


def shards(densities, trials, energies, metric, pair_local, pair_remote, pair_scale):
    mols = densities.shape[2]
    states = energies.shape[3]
    aux = metric.shape[0]
    field = trials.shape[3]
    pairs = pair_local.shape[2]
    width = mols * states
    nx, ny = lax.axis_size("gx"), lax.axis_size("gy")

    def spot(x, y):
        return (x % nx) * ny + y % ny

    def take(value, dx, dy, only=lambda x, y: True):
        table = [
            (spot(x + dx, y + dy), spot(x, y))
            for x in range(nx)
            for y in range(ny)
            if only(x, y)
        ]
        return lax.ppermute(value, AXES, table)

    def butterfly(value):
        step = 1
        while step < ny:
            value = value + lax.ppermute(
                value, AXES, [(spot(x, y ^ step), spot(x, y)) for x in range(nx) for y in range(ny)]
            )
            step *= 2
        step = 1
        while step < nx:
            value = value + lax.ppermute(
                value, AXES, [(spot(x ^ step, y), spot(x, y)) for x in range(nx) for y in range(ny)]
            )
            step *= 2
        return value

    rho_a, y_a, e_a = densities[0, 0], trials[0, 0], energies[0, 0]
    rho_r = take(rho_a, 1, 0)
    rho_u = take(rho_a, 0, 1)

    own, msg = call(
        functools.partial(weights_body, aux**-0.5),
        (shape(4, mols, 2 * mols), shape(3, mols, field + 4 * mols)),
        9 * 2 * 3 * mols * 2 * mols * (pairs // 9),
        12 * pairs,
    )(pair_local[0], pair_remote[0], pair_scale[0], y_a, e_a)
    msg_r = take(msg[0], 1, 0)
    msg_u = take(msg[1], 0, 1)
    msg_c = take(msg[2], 1, 1)

    near = take(rho_r, 0, 1, lambda x, y: y % 2 == 0)
    far = take(rho_u, 1, 0, lambda x, y: y % 2 == 1)
    rho_c = jnp.where(lax.axis_index("gy") % 2 == 0, near, far)

    block = 2 * width * width * aux
    proj = 2 * width * aux * aux
    size = width * aux * 2
    proj_a, c_aa = call(
        functools.partial(self_body, states),
        (shape(width, aux, dtype=BF), shape(width, width, dtype=BF)),
        proj + block,
        4 * size,
    )(rho_a, metric, own)
    proj_r, c_r = call(
        functools.partial(right_body, states),
        (shape(width, aux, dtype=BF), shape(2, width, width, dtype=BF)),
        proj + 2 * block,
        6 * size,
    )(rho_a, rho_r, metric, proj_a, own, msg_r)
    c_u, sig = call(
        functools.partial(up_body, states),
        (shape(4, width, width, dtype=BF), shape(3, width, field // states)),
        proj + 4 * block,
        9 * size,
    )(rho_a, rho_r, rho_u, metric, proj_a, proj_r, own, msg_r, msg_u, c_aa, c_r, y_a)
    c_c, parts, sums = call(
        functools.partial(corner_body, states),
        (shape(2, width, width, dtype=BF), shape(4, mols, field), shape(2, field)),
        proj + 2 * block,
        6 * size,
    )(rho_a, rho_c, metric, proj_a, own, msg_r, msg_u, msg_c, y_a, e_a, sig)

    def home(parts):
        below = take(parts[2:4], 0, -1)
        left = take(parts[1] + below[1], -1, 0)
        return (parts[0] + below[0]) + left

    sums = butterfly(sums)
    sigma = home(parts)
    sig_r = take(sigma, 1, 0)
    upper = take(jnp.stack([sigma, sig_r]), 0, 1)
    theta, resid, squares = call(
        functools.partial(theta_body, states),
        (shape(1, field), shape(mols, field), shape(1, field)),
        20 * mols * field,
        12 * mols * field,
    )(sums, sigma, y_a, e_a)
    parts2 = call(
        functools.partial(second_body, states),
        shape(4, mols, field),
        9 * 2 * width * field * mols,
        9 * width * width * 2,
    )(theta, resid, sig_r, upper[0], upper[1], msg_r, msg_u, msg_c, c_aa, c_r, c_u, c_c)
    squares = butterfly(squares)
    corr, sigma2 = call(
        functools.partial(last_body, states, float(width * nx * ny)),
        (shape(mols, field, dtype=BF), shape(mols, field)),
        20 * mols * field,
        16 * mols * field,
    )(squares, resid, home(parts2), e_a)
    out = (1, 1, mols, field)
    return (
        sigma.reshape(out),
        corr.reshape(out),
        sigma2.reshape(out),
        theta[0, : field // states],
    )


def solution(mesh):
    return jax.shard_map(
        shards,
        mesh=mesh,
        in_specs=(
            P("gx", "gy", None, None),
            P("gx", "gy", None, None),
            P("gx", "gy", None, None),
            P(),
            P("gx", "gy", None),
            P("gx", "gy", None),
            P("gx", "gy", None),
        ),
        out_specs=(
            P("gx", "gy", None, None),
            P("gx", "gy", None, None),
            P("gx", "gy", None, None),
            P(),
        ),
        check_vma=False,
    )
```

```python
import functools

import jax
import jax.numpy as jnp
from jax import lax
from jax.experimental import pallas as pl
from jax.experimental.pallas import tpu as pltpu
from jax.sharding import PartitionSpec as P


BF = jnp.bfloat16
F32 = jnp.float32
AXES = ("gx", "gy")
SELF, TO_R, TO_U, TO_UR = 4, 7, 5, 8
R_TO_A, R_TO_U, U_TO_A, U_TO_R, UR_TO_A = 1, 2, 3, 6, 0


def vmem(count):
    return [pl.BlockSpec(memory_space=pltpu.VMEM)] * count


def call(body, outs, flops, moved, smem=0):
    return lambda *args: pl.pallas_call(
        body,
        out_shape=outs,
        in_specs=[pl.BlockSpec(memory_space=pltpu.SMEM)] * smem + vmem(len(args) - smem),
        out_specs=jax.tree.map(lambda _: pl.BlockSpec(memory_space=pltpu.VMEM), outs),
        compiler_params=pltpu.CompilerParams(vmem_limit_bytes=60 * 2**20),
        cost_estimate=pl.CostEstimate(flops=flops, bytes_accessed=moved, transcendentals=0),
    )(*args)


def shape(*dims, dtype=F32):
    return jax.ShapeDtypeStruct(dims, dtype)


def stack(ref, states):
    width = ref.shape[1] // states
    return jnp.concatenate([ref[:, a * width : (a + 1) * width] for a in range(states)], axis=0)


def unstack(value, states):
    mols = value.shape[0] // states
    return jnp.concatenate([value[a * mols : (a + 1) * mols] for a in range(states)], axis=1)


def dot_nt(a, b):
    return lax.dot_general(a, b, (((1,), (1,)), ((), ())), preferred_element_type=F32)


def dot(a, b):
    return jnp.dot(a, b, preferred_element_type=F32)


def twice(w):
    return jnp.concatenate([w, w], axis=1)


def couple(proj, rho, pair):
    dense = dot_nt(proj, rho)
    tiles = (dense.shape[0] // pair.shape[0], dense.shape[1] // pair.shape[1])
    return (dense * jnp.tile(pair, tiles)).astype(BF)


def spread(e, width):
    mols, states = e.shape
    lane = lax.broadcasted_iota(jnp.int32, (mols, states * width), 1) // width
    out = jnp.zeros((mols, states * width), F32)
    for a in range(states):
        out = jnp.where(lane == a, e[:, a : a + 1], out)
    return out


def weights_body(scale, loc, rem, sc, y, e, own_a, own_r, own_u, own_c, msg_r, msg_u, msg_c):
    mols = y.shape[0]
    cap = loc.shape[1] // 9
    mol = lax.broadcasted_iota(jnp.int32, (mols, cap), 0)

    def weight(o):
        part = slice(o * cap, (o + 1) * cap)
        left, right, factor = loc[:, part], rem[:, part], sc[:, part] * scale
        if o == 4:
            right = left + 1 + right
            right = jnp.where(right >= mols, right - mols, right)
        mine = jnp.where(mol == left, factor, 0.0)
        far = jnp.where(mol == right, 1.0, 0.0).astype(BF)
        high = mine.astype(BF)
        rest = mine - high.astype(F32)
        mid = rest.astype(BF)
        low = (rest - mid.astype(F32)).astype(BF)
        three = dot_nt(
            jnp.concatenate([high, mid, low], axis=0), jnp.concatenate([far, far], axis=0)
        )
        return three[:mols] + (three[mols : 2 * mols] + three[2 * mols :])

    for own, o in ((own_a, SELF), (own_r, TO_R), (own_u, TO_U), (own_c, TO_UR)):
        own[...] = weight(o)
    field = y.shape[1]
    for msg, o, q in (
        (msg_r, R_TO_A, R_TO_U),
        (msg_u, U_TO_A, U_TO_R),
        (msg_c, UR_TO_A, None),
    ):
        first = weight(o)
        if q is not None:
            lane = lax.broadcasted_iota(jnp.int32, first.shape, 1)
            first = jnp.where(lane < mols, first, weight(q))
        msg[:, :field] = y[...].astype(F32)
        msg[:, field : field + 2 * mols] = first
        msg[:, field + 2 * mols :] = jnp.concatenate(
            [e[...], jnp.zeros((mols, 2 * mols - e.shape[1]), F32)], axis=1
        )


def self_body(states, rho, metric, own, proj, c_aa):
    rows = stack(rho, states)
    proj[...] = dot(rows, metric[...]).astype(BF)
    c_aa[...] = couple(proj[...], rows, own[...])


def right_body(states, rho_a, rho_r, metric, proj_a, own, msg_r, proj_r, c):
    mols = rho_a.shape[0]
    rows_a, rows_r = stack(rho_a, states), stack(rho_r, states)
    field = msg_r.shape[1] - 4 * mols
    c[0] = couple(proj_a[...], rows_r, own[...])
    proj_r[...] = dot(rows_r, metric[...]).astype(BF)
    c[1] = couple(proj_r[...], rows_a, twice(msg_r[:, field : field + mols]))


def up_body(
    states, rho_a, rho_r, rho_u, metric, proj_a, proj_r, own, msg_r, msg_u, c_aa, c_r, y_a, c, sig
):
    mols = rho_a.shape[0]
    field = msg_r.shape[1] - 4 * mols
    rows_u = stack(rho_u, states)
    c[0] = couple(proj_a[...], rows_u, own[...])
    c[1] = couple(proj_r[...], rows_u, twice(msg_r[:, field + mols : field + 2 * mols]))
    proj_u = dot(rows_u, metric[...]).astype(BF)
    c[2] = couple(proj_u, stack(rho_a, states), twice(msg_u[:, field : field + mols]))
    c[3] = couple(
        proj_u, stack(rho_r, states), twice(msg_u[:, field + mols : field + 2 * mols])
    )
    f_a = stack(y_a, states)
    f_r = stack(msg_r[:, :field], states).astype(BF)
    f_u = stack(msg_u[:, :field], states).astype(BF)
    sig[0] = dot(c_aa[...], f_a) + (dot(c_r[0], f_r) + dot(c[0], f_u))
    sig[1] = dot(c_r[1], f_a) + dot(c[1], f_u)
    sig[2] = dot(c[2], f_a) + dot(c[3], f_r)


def corner_body(
    states,
    second,
    rho_a,
    near,
    far,
    metric,
    proj_a,
    own,
    msg_r,
    msg_u,
    msg_c,
    y_a,
    e_a,
    sig,
    c,
    to_a,
    to_r,
    to_uc,
    sums,
):
    mols = rho_a.shape[0]
    field = msg_r.shape[1] - 4 * mols
    width = near.shape[1] // states
    pick = second[0, 0] == 1
    rows_c = jnp.concatenate(
        [
            jnp.where(pick, far[:, a * width : (a + 1) * width], near[:, a * width : (a + 1) * width])
            for a in range(states)
        ],
        axis=0,
    )
    c[0] = couple(proj_a[...], rows_c, own[...])
    proj_c = dot(rows_c, metric[...]).astype(BF)
    c[1] = couple(proj_c, stack(rho_a, states), twice(msg_c[:, field : field + mols]))
    f_a = stack(y_a, states)
    f_c = stack(msg_c[:, :field], states).astype(BF)
    own_y = y_a[...].astype(F32)
    part_a = unstack(sig[0] + dot(c[0], f_c), states)
    part_a = part_a + spread(e_a[...], field // states) * own_y
    part_r = unstack(sig[1], states)
    part_u = unstack(sig[2], states)
    part_c = unstack(dot(c[1], f_a), states)
    to_a[...], to_r[...], to_uc[0], to_uc[1] = part_a, part_r, part_u, part_c
    total = part_a * own_y + part_r * msg_r[:, :field]
    total = total + (part_u * msg_u[:, :field] + part_c * msg_c[:, :field])
    sums[0:1] = jnp.sum(total, axis=0, keepdims=True)
    sums[1:2] = jnp.sum(own_y * own_y, axis=0, keepdims=True)


def over_states(row, width):
    states = row.shape[1] // width
    total = row[:, :width]
    for a in range(1, states):
        total = total + row[:, a * width : (a + 1) * width]
    return jnp.concatenate([total] * states, axis=1)


def residual(sigma, y, e, theta, width):
    return (sigma - theta * y) / jnp.maximum(jnp.abs(spread(e, width) - theta), 1.0)


def theta_body(states, sums, sigma, y_a, e_a, theta, resid, squares):
    width = sigma.shape[1] // states
    rate = over_states(sums[0:1], width) / over_states(sums[1:2], width)
    theta[...] = rate
    value = residual(sigma[...], y_a[...].astype(F32), e_a[...], rate, width)
    resid[...] = value
    squares[...] = jnp.sum(value * value, axis=0, keepdims=True)


def second_body(
    states, theta, resid, sig_r, sig_uc, msg_r, msg_u, msg_c, c_aa, c_r, c_u, c_c, to_a, to_r, to_uc
):
    mols, field = resid.shape
    width = field // states

    def other(sigma, msg):
        e = msg[:, field + 2 * mols : field + 2 * mols + states]
        value = residual(sigma, msg[:, :field], e, theta[...], width)
        return stack(value, states).astype(BF)

    f_a = stack(resid[...], states).astype(BF)
    f_r = other(sig_r[...], msg_r)
    f_u = other(sig_uc[0], msg_u)
    f_c = other(sig_uc[1], msg_c)
    row_a = (dot(c_aa[...], f_a) + dot(c_r[0], f_r)) + (dot(c_u[0], f_u) + dot(c_c[0], f_c))
    to_a[...] = unstack(row_a, states)
    to_r[...] = unstack(dot(c_r[1], f_a) + dot(c_u[1], f_u), states)
    to_uc[0] = unstack(dot(c_u[2], f_a) + dot(c_u[3], f_r), states)
    to_uc[1] = unstack(dot(c_c[1], f_a), states)


def last_body(states, count, squares, resid, raw, e_a, corr, sigma):
    width = resid.shape[1] // states
    scale = jnp.sqrt(over_states(squares[...], width) / count + 1e-06)
    value = (resid[...] / scale).astype(BF)
    corr[...] = value
    sigma[...] = raw[...] / scale + spread(e_a[...], width) * value.astype(F32)


def shards(densities, trials, energies, metric, pair_local, pair_remote, pair_scale):
    mols = densities.shape[2]
    states = energies.shape[3]
    aux = metric.shape[0]
    field = trials.shape[3]
    pairs = pair_local.shape[2]
    width = mols * states
    nx, ny = lax.axis_size("gx"), lax.axis_size("gy")

    def spot(x, y):
        return (x % nx) * ny + y % ny

    def take(value, dx, dy, only=lambda x, y: True):
        table = [
            (spot(x + dx, y + dy), spot(x, y))
            for x in range(nx)
            for y in range(ny)
            if only(x, y)
        ]
        return lax.ppermute(value, AXES, table)

    flips = [(0, 2), (1, 0), (2, 0), (0, 4), (0, 8), (4, 0), (8, 0), (0, 1)]

    def butterfly(value):
        for fx, fy in flips:
            table = [(spot(x ^ fx, y ^ fy), spot(x, y)) for x in range(nx) for y in range(ny)]
            value = value + lax.ppermute(value, AXES, table)
        return value

    rho_a, y_a, e_a = densities[0, 0], trials[0, 0], energies[0, 0]
    rho_r = take(rho_a, 1, 0)
    rho_u = take(rho_a, 0, 1)

    pair = shape(mols, 2 * mols)
    note = shape(mols, field + 4 * mols)
    own_a, own_r, own_u, own_c, msg_r, msg_u, msg_c = call(
        functools.partial(weights_body, aux**-0.5),
        (pair, pair, pair, pair, note, note, note),
        9 * 2 * 3 * mols * 2 * mols * (pairs // 9),
        12 * pairs,
    )(pair_local[0], pair_remote[0], pair_scale[0], y_a, e_a)
    msg_r = take(msg_r, 1, 0)
    msg_u = take(msg_u, 0, 1)
    msg_c = take(msg_c, 1, 1)

    near = take(rho_r, 0, 1, lambda x, y: y % 2 == 0)
    far = take(rho_u, 1, 0, lambda x, y: y % 2 == 1)

    block = 2 * width * width * aux
    proj = 2 * width * aux * aux
    size = width * aux * 2
    proj_a, c_aa = call(
        functools.partial(self_body, states),
        (shape(width, aux, dtype=BF), shape(width, width, dtype=BF)),
        proj + block,
        4 * size,
    )(rho_a, metric, own_a)
    proj_r, c_r = call(
        functools.partial(right_body, states),
        (shape(width, aux, dtype=BF), shape(2, width, width, dtype=BF)),
        proj + 2 * block,
        6 * size,
    )(rho_a, rho_r, metric, proj_a, own_r, msg_r)
    c_u, sig = call(
        functools.partial(up_body, states),
        (shape(4, width, width, dtype=BF), shape(3, width, field // states)),
        proj + 4 * block,
        9 * size,
    )(rho_a, rho_r, rho_u, metric, proj_a, proj_r, own_u, msg_r, msg_u, c_aa, c_r, y_a)
    one, two = shape(mols, field), shape(2, mols, field)
    second = (lax.axis_index("gy") % 2).astype(jnp.int32).reshape(1, 1)
    c_c, to_a, to_r, to_uc, sums = call(
        functools.partial(corner_body, states),
        (shape(2, width, width, dtype=BF), one, one, two, shape(2, field)),
        proj + 2 * block,
        6 * size,
        smem=1,
    )(second, rho_a, near, far, metric, proj_a, own_c, msg_r, msg_u, msg_c, y_a, e_a, sig)

    def home(to_a, to_r, to_uc):
        below = take(to_uc, 0, -1)
        left = take(to_r + below[1], -1, 0)
        return (to_a + below[0]) + left

    sums = butterfly(sums)
    sigma = home(to_a, to_r, to_uc)
    sig_r = take(sigma, 1, 0)
    sig_uc = take(jnp.stack([sigma, sig_r]), 0, 1)
    theta, resid, squares = call(
        functools.partial(theta_body, states),
        (shape(1, field), one, shape(1, field)),
        20 * mols * field,
        12 * mols * field,
    )(sums, sigma, y_a, e_a)
    to_a, to_r, to_uc = call(
        functools.partial(second_body, states),
        (one, one, two),
        9 * 2 * width * field * mols,
        9 * width * width * 2,
    )(theta, resid, sig_r, sig_uc, msg_r, msg_u, msg_c, c_aa, c_r, c_u, c_c)
    squares = butterfly(squares)
    raw = home(to_a, to_r, to_uc)
    corr, sigma2 = call(
        functools.partial(last_body, states, float(width * nx * ny)),
        (shape(mols, field, dtype=BF), one),
        20 * mols * field,
        16 * mols * field,
    )(squares, resid, raw, e_a)
    out = (1, 1, mols, field)
    return (
        sigma.reshape(out),
        corr.reshape(out),
        sigma2.reshape(out),
        theta[0, : field // states],
    )


def solution(mesh):
    return jax.shard_map(
        shards,
        mesh=mesh,
        in_specs=(
            P("gx", "gy", None, None),
            P("gx", "gy", None, None),
            P("gx", "gy", None, None),
            P(),
            P("gx", "gy", None),
            P("gx", "gy", None),
            P("gx", "gy", None),
        ),
        out_specs=(
            P("gx", "gy", None, None),
            P("gx", "gy", None, None),
            P("gx", "gy", None, None),
            P(),
        ),
        check_vma=False,
    )
```

```python
import functools

import jax
import jax.numpy as jnp
from jax import lax
from jax.experimental import pallas as pl
from jax.experimental.pallas import tpu as pltpu
from jax.sharding import PartitionSpec as P


BF = jnp.bfloat16
F32 = jnp.float32
AXES = ("gx", "gy")
SELF, TO_R, TO_U, TO_UR = 4, 7, 5, 8
R_TO_A, R_TO_U, U_TO_A, U_TO_R, UR_TO_A = 1, 2, 3, 6, 0


def vmem(count):
    return [pl.BlockSpec(memory_space=pltpu.VMEM)] * count


def call(body, outs, flops, moved, smem=0, limit=24):
    return lambda *args: pl.pallas_call(
        body,
        out_shape=outs,
        in_specs=[pl.BlockSpec(memory_space=pltpu.SMEM)] * smem + vmem(len(args) - smem),
        out_specs=jax.tree.map(lambda _: pl.BlockSpec(memory_space=pltpu.VMEM), outs),
        compiler_params=pltpu.CompilerParams(vmem_limit_bytes=limit * 2**20),
        cost_estimate=pl.CostEstimate(flops=flops, bytes_accessed=moved, transcendentals=0),
    )(*args)


def shape(*dims, dtype=F32):
    return jax.ShapeDtypeStruct(dims, dtype)


def stack(ref, states):
    width = ref.shape[1] // states
    return jnp.concatenate([ref[:, a * width : (a + 1) * width] for a in range(states)], axis=0)


def unstack(value, states):
    mols = value.shape[0] // states
    return jnp.concatenate([value[a * mols : (a + 1) * mols] for a in range(states)], axis=1)


def dot_nt(a, b):
    return lax.dot_general(a, b, (((1,), (1,)), ((), ())), preferred_element_type=F32)


def dot(a, b):
    return jnp.dot(a, b, preferred_element_type=F32)


def twice(w):
    return jnp.concatenate([w, w], axis=1)


def couple(proj, rho, pair):
    dense = dot_nt(proj, rho)
    tiles = (dense.shape[0] // pair.shape[0], dense.shape[1] // pair.shape[1])
    return (dense * jnp.tile(pair, tiles)).astype(BF)


def spread(e, width):
    mols, states = e.shape
    lane = lax.broadcasted_iota(jnp.int32, (mols, states * width), 1) // width
    out = jnp.zeros((mols, states * width), F32)
    for a in range(states):
        out = jnp.where(lane == a, e[:, a : a + 1], out)
    return out


def weights_body(scale, loc, rem, sc, y, e, own_a, own_r, own_u, own_c, msg_r, msg_u, msg_c):
    mols = y.shape[0]
    cap = loc.shape[1] // 9
    mol = lax.broadcasted_iota(jnp.int32, (mols, cap), 0)

    def weight(o):
        part = slice(o * cap, (o + 1) * cap)
        left, right, factor = loc[:, part], rem[:, part], sc[:, part] * scale
        if o == 4:
            right = left + 1 + right
            right = jnp.where(right >= mols, right - mols, right)
        mine = jnp.where(mol == left, factor, 0.0)
        far = jnp.where(mol == right, 1.0, 0.0).astype(BF)
        high = mine.astype(BF)
        rest = mine - high.astype(F32)
        mid = rest.astype(BF)
        low = (rest - mid.astype(F32)).astype(BF)
        three = dot_nt(
            jnp.concatenate([high, mid, low], axis=0), jnp.concatenate([far, far], axis=0)
        )
        return three[:mols] + (three[mols : 2 * mols] + three[2 * mols :])

    for own, o in ((own_a, SELF), (own_r, TO_R), (own_u, TO_U), (own_c, TO_UR)):
        own[...] = weight(o)
    field = y.shape[1]
    for msg, o, q in (
        (msg_r, R_TO_A, R_TO_U),
        (msg_u, U_TO_A, U_TO_R),
        (msg_c, UR_TO_A, None),
    ):
        first = weight(o)
        if q is not None:
            lane = lax.broadcasted_iota(jnp.int32, first.shape, 1)
            first = jnp.where(lane < mols, first, weight(q))
        msg[:, :field] = y[...].astype(F32)
        msg[:, field : field + 2 * mols] = first
        msg[:, field + 2 * mols :] = jnp.concatenate(
            [e[...], jnp.zeros((mols, 2 * mols - e.shape[1]), F32)], axis=1
        )


def self_body(states, rho, metric, own, proj, c_aa):
    rows = stack(rho, states)
    proj[...] = dot(rows, metric[...]).astype(BF)
    c_aa[...] = couple(proj[...], rows, own[...])


def first_body(states, rho_a, rho_u, metric, proj_a, own, msg_u, proj_u, c):
    mols = rho_a.shape[0]
    field = msg_u.shape[1] - 4 * mols
    rows_a, rows_u = stack(rho_a, states), stack(rho_u, states)
    c[0] = couple(proj_a[...], rows_u, own[...])
    proj_u[...] = dot(rows_u, metric[...]).astype(BF)
    c[1] = couple(proj_u[...], rows_a, twice(msg_u[:, field : field + mols]))


def next_body(
    states, rho_a, rho_u, rho_r, metric, proj_a, proj_u, own, msg_u, msg_r, c_aa, c_u, y_a, c, sig
):
    mols = rho_a.shape[0]
    field = msg_r.shape[1] - 4 * mols
    rows_r = stack(rho_r, states)
    c[0] = couple(proj_a[...], rows_r, own[...])
    c[1] = couple(proj_u[...], rows_r, twice(msg_u[:, field + mols : field + 2 * mols]))
    proj_r = dot(rows_r, metric[...]).astype(BF)
    c[2] = couple(proj_r, stack(rho_a, states), twice(msg_r[:, field : field + mols]))
    c[3] = couple(
        proj_r, stack(rho_u, states), twice(msg_r[:, field + mols : field + 2 * mols])
    )
    f_a = stack(y_a, states)
    f_r = stack(msg_r[:, :field], states).astype(BF)
    f_u = stack(msg_u[:, :field], states).astype(BF)
    sig[0] = dot(c_aa[...], f_a) + (dot(c_u[0], f_u) + dot(c[0], f_r))
    sig[1] = dot(c[2], f_a) + dot(c[3], f_u)
    sig[2] = dot(c_u[1], f_a) + dot(c[1], f_r)


def corner_body(
    states,
    second,
    rho_a,
    near,
    far,
    metric,
    proj_a,
    own,
    msg_r,
    msg_u,
    msg_c,
    y_a,
    e_a,
    sig,
    c,
    to_a,
    to_r,
    to_uc,
    sums,
):
    mols = rho_a.shape[0]
    field = msg_r.shape[1] - 4 * mols
    width = near.shape[1] // states
    pick = second[0, 0] == 1
    rows_c = jnp.concatenate(
        [
            jnp.where(pick, far[:, a * width : (a + 1) * width], near[:, a * width : (a + 1) * width])
            for a in range(states)
        ],
        axis=0,
    )
    c[0] = couple(proj_a[...], rows_c, own[...])
    proj_c = dot(rows_c, metric[...]).astype(BF)
    c[1] = couple(proj_c, stack(rho_a, states), twice(msg_c[:, field : field + mols]))
    f_a = stack(y_a, states)
    f_c = stack(msg_c[:, :field], states).astype(BF)
    own_y = y_a[...].astype(F32)
    part_a = unstack(sig[0] + dot(c[0], f_c), states)
    part_a = part_a + spread(e_a[...], field // states) * own_y
    part_r = unstack(sig[1], states)
    part_u = unstack(sig[2], states)
    part_c = unstack(dot(c[1], f_a), states)
    to_a[...], to_r[...], to_uc[0], to_uc[1] = part_a, part_r, part_u, part_c
    total = part_a * own_y + part_r * msg_r[:, :field]
    total = total + (part_u * msg_u[:, :field] + part_c * msg_c[:, :field])
    sums[0:1] = jnp.sum(total, axis=0, keepdims=True)
    sums[1:2] = jnp.sum(own_y * own_y, axis=0, keepdims=True)


def over_states(row, width):
    states = row.shape[1] // width
    total = row[:, :width]
    for a in range(1, states):
        total = total + row[:, a * width : (a + 1) * width]
    return jnp.concatenate([total] * states, axis=1)


def residual(sigma, y, e, theta, width):
    return (sigma - theta * y) / jnp.maximum(jnp.abs(spread(e, width) - theta), 1.0)


def theta_body(states, part, rest, sigma, y_a, e_a, theta, short, resid, squares):
    width = sigma.shape[1] // states
    sums = part[...] + rest[...]
    rate = over_states(sums[0:1], width) / over_states(sums[1:2], width)
    theta[...] = rate
    short[...] = rate[:, :width]
    value = residual(sigma[...], y_a[...].astype(F32), e_a[...], rate, width)
    resid[...] = value
    squares[...] = jnp.sum(value * value, axis=0, keepdims=True)


def second_body(
    states, theta, resid, sig_r, sig_uc, msg_r, msg_u, msg_c, c_aa, c_r, c_u, c_c, to_a, to_r, to_uc
):
    mols, field = resid.shape
    width = field // states

    def other(sigma, msg):
        e = msg[:, field + 2 * mols : field + 2 * mols + states]
        value = residual(sigma, msg[:, :field], e, theta[...], width)
        return stack(value, states).astype(BF)

    f_a = stack(resid[...], states).astype(BF)
    f_r = other(sig_r[...], msg_r)
    f_u = other(sig_uc[0], msg_u)
    f_c = other(sig_uc[1], msg_c)
    row_a = (dot(c_aa[...], f_a) + dot(c_u[0], f_u)) + (dot(c_r[0], f_r) + dot(c_c[0], f_c))
    to_a[...] = unstack(row_a, states)
    to_r[...] = unstack(dot(c_r[2], f_a) + dot(c_r[3], f_u), states)
    to_uc[0] = unstack(dot(c_u[1], f_a) + dot(c_r[1], f_r), states)
    to_uc[1] = unstack(dot(c_c[1], f_a), states)


def last_body(states, count, part, rest, resid, to_a, below, left, e_a, corr, sigma):
    width = resid.shape[1] // states
    scale = jnp.sqrt(over_states(part[...] + rest[...], width) / count + 1e-06)
    value = (resid[...] / scale).astype(BF)
    corr[...] = value
    raw = (to_a[...] + below[0]) + left[...]
    sigma[...] = raw / scale + spread(e_a[...], width) * value.astype(F32)


def shards(densities, trials, energies, metric, pair_local, pair_remote, pair_scale):
    mols = densities.shape[2]
    states = energies.shape[3]
    aux = metric.shape[0]
    field = trials.shape[3]
    pairs = pair_local.shape[2]
    width = mols * states
    nx, ny = lax.axis_size("gx"), lax.axis_size("gy")

    def spot(x, y):
        return (x % nx) * ny + y % ny

    def take(value, dx, dy, only=lambda x, y: True):
        table = [
            (spot(x + dx, y + dy), spot(x, y))
            for x in range(nx)
            for y in range(ny)
            if only(x, y)
        ]
        return lax.ppermute(value, AXES, table)

    def along_z(table):
        def partner(x, y):
            z = table[(y // 2 % 2) * 4 + x % 4]
            return x // 4 * 4 + z % 4, y // 4 * 4 + z // 4 * 2 + y % 2

        return partner

    def flip(fx, fy):
        return lambda x, y: (x ^ fx, y ^ fy)

    steps = [
        along_z((3, 6, 5, 0, 7, 2, 1, 4)),
        along_z((7, 2, 1, 4, 3, 6, 5, 0)),
        along_z((1, 0, 3, 2, 5, 4, 7, 6)),
        flip(0, 4),
        flip(0, 12),
        flip(4, 0),
        flip(12, 0),
        flip(0, 1),
    ]

    def butterfly(value):
        for k, partner in enumerate(steps):
            table = [(spot(*partner(x, y)), spot(x, y)) for x in range(nx) for y in range(ny)]
            other = lax.ppermute(value, AXES, table)
            if k == len(steps) - 1:
                return value, other
            value = value + other

    rho_a, y_a, e_a = densities[0, 0], trials[0, 0], energies[0, 0]
    rho_u = take(rho_a, 0, 1)

    pair = shape(mols, 2 * mols)
    note = shape(mols, field + 4 * mols)
    own_a, own_r, own_u, own_c, msg_r, msg_u, msg_c = call(
        functools.partial(weights_body, aux**-0.5),
        (pair, pair, pair, pair, note, note, note),
        9 * 2 * 3 * mols * 2 * mols * (pairs // 9),
        12 * pairs,
    )(pair_local[0], pair_remote[0], pair_scale[0], y_a, e_a)
    msg_r = take(msg_r, 1, 0)
    msg_u = take(msg_u, 0, 1)
    msg_c = take(msg_c, 1, 1)

    rho_r = take(rho_a, 1, 0)
    near = take(rho_r, 0, 1, lambda x, y: y % 2 == 0)
    far = take(rho_u, 1, 0, lambda x, y: y % 2 == 1)

    block = 2 * width * width * aux
    proj = 2 * width * aux * aux
    size = width * aux * 2
    proj_a, c_aa = call(
        functools.partial(self_body, states),
        (shape(width, aux, dtype=BF), shape(width, width, dtype=BF)),
        proj + block,
        4 * size,
    )(rho_a, metric, own_a)
    proj_u, c_u = call(
        functools.partial(first_body, states),
        (shape(width, aux, dtype=BF), shape(2, width, width, dtype=BF)),
        proj + 2 * block,
        6 * size,
    )(rho_a, rho_u, metric, proj_a, own_u, msg_u)
    c_r, sig = call(
        functools.partial(next_body, states),
        (shape(4, width, width, dtype=BF), shape(3, width, field // states)),
        proj + 4 * block,
        9 * size,
    )(rho_a, rho_u, rho_r, metric, proj_a, proj_u, own_r, msg_u, msg_r, c_aa, c_u, y_a)
    one, two = shape(mols, field), shape(2, mols, field)
    second = (lax.axis_index("gy") % 2).astype(jnp.int32).reshape(1, 1)
    c_c, to_a, to_r, to_uc, sums = call(
        functools.partial(corner_body, states),
        (shape(2, width, width, dtype=BF), one, one, two, shape(2, field)),
        proj + 2 * block,
        6 * size,
        smem=1,
    )(second, rho_a, near, far, metric, proj_a, own_c, msg_r, msg_u, msg_c, y_a, e_a, sig)

    def home(to_r, to_uc):
        below = take(to_uc, 0, -1)
        left = take(to_r + below[1], -1, 0)
        return below, left

    sums = butterfly(sums)
    below, left = home(to_r, to_uc)
    sigma = (to_a + below[0]) + left
    sig_r = take(sigma, 1, 0)
    sig_uc = take(jnp.stack([sigma, sig_r]), 0, 1)
    theta, short, resid, squares = call(
        functools.partial(theta_body, states),
        (shape(1, field), shape(1, field // states), one, shape(1, field)),
        20 * mols * field,
        12 * mols * field,
    )(*sums, sigma, y_a, e_a)
    to_a, to_r, to_uc = call(
        functools.partial(second_body, states),
        (one, one, two),
        9 * 2 * width * field * mols,
        9 * width * width * 2,
    )(theta, resid, sig_r, sig_uc, msg_r, msg_u, msg_c, c_aa, c_r, c_u, c_c)
    squares = butterfly(squares)
    below, left = home(to_r, to_uc)
    corr, sigma2 = call(
        functools.partial(last_body, states, float(width * nx * ny)),
        (shape(mols, field, dtype=BF), one),
        20 * mols * field,
        16 * mols * field,
    )(*squares, resid, to_a, below, left, e_a)
    out = (1, 1, mols, field)
    return (
        sigma.reshape(out),
        corr.reshape(out),
        sigma2.reshape(out),
        short.reshape(field // states),
    )


def solution(mesh):
    return jax.shard_map(
        shards,
        mesh=mesh,
        in_specs=(
            P("gx", "gy", None, None),
            P("gx", "gy", None, None),
            P("gx", "gy", None, None),
            P(),
            P("gx", "gy", None),
            P("gx", "gy", None),
            P("gx", "gy", None),
        ),
        out_specs=(
            P("gx", "gy", None, None),
            P("gx", "gy", None, None),
            P("gx", "gy", None, None),
            P(),
        ),
        check_vma=False,
    )
```

```python
import functools

import jax
import jax.numpy as jnp
from jax import lax
from jax.experimental import pallas as pl
from jax.experimental.pallas import tpu as pltpu
from jax.sharding import PartitionSpec as P


BF = jnp.bfloat16
F32 = jnp.float32
AXES = ("gx", "gy")
SELF, TO_R, TO_U, TO_UR = 4, 7, 5, 8
R_TO_A, R_TO_U, U_TO_A, U_TO_R, UR_TO_A = 1, 2, 3, 6, 0


def vmem(count):
    return [pl.BlockSpec(memory_space=pltpu.VMEM)] * count


def call(body, outs, flops, moved, smem=0, scratch=()):
    return lambda *args: pl.pallas_call(
        body,
        out_shape=outs,
        in_specs=[pl.BlockSpec(memory_space=pltpu.SMEM)] * smem + vmem(len(args) - smem),
        out_specs=jax.tree.map(lambda _: pl.BlockSpec(memory_space=pltpu.VMEM), outs),
        scratch_shapes=scratch,
        compiler_params=pltpu.CompilerParams(vmem_limit_bytes=24 * 2**20),
        cost_estimate=pl.CostEstimate(flops=flops, bytes_accessed=moved, transcendentals=0),
    )(*args)


def shape(*dims, dtype=F32):
    return jax.ShapeDtypeStruct(dims, dtype)


def stack(ref, states):
    width = ref.shape[1] // states
    return jnp.concatenate([ref[:, a * width : (a + 1) * width] for a in range(states)], axis=0)


def unstack(value, states):
    mols = value.shape[0] // states
    return jnp.concatenate([value[a * mols : (a + 1) * mols] for a in range(states)], axis=1)


def dot_nt(a, b):
    return lax.dot_general(a, b, (((1,), (1,)), ((), ())), preferred_element_type=F32)


def dot(a, b):
    return jnp.dot(a, b, preferred_element_type=F32)


def twice(w):
    return jnp.concatenate([w, w], axis=1)


def couple(proj, rho, pair):
    dense = dot_nt(proj, rho)
    tiles = (dense.shape[0] // pair.shape[0], dense.shape[1] // pair.shape[1])
    return (dense * jnp.tile(pair, tiles)).astype(BF)


def spread(e, width):
    mols, states = e.shape
    lane = lax.broadcasted_iota(jnp.int32, (mols, states * width), 1) // width
    out = jnp.zeros((mols, states * width), F32)
    for a in range(states):
        out = jnp.where(lane == a, e[:, a : a + 1], out)
    return out


def weights_body(scale, loc, rem, sc, y, e, own_a, own_r, own_u, own_c, msg_r, msg_u, msg_c):
    mols = y.shape[0]
    cap = loc.shape[1] // 9
    mol = lax.broadcasted_iota(jnp.int32, (mols, cap), 0)

    def weight(o):
        part = slice(o * cap, (o + 1) * cap)
        left, right, factor = loc[:, part], rem[:, part], sc[:, part] * scale
        if o == 4:
            right = left + 1 + right
            right = jnp.where(right >= mols, right - mols, right)
        mine = jnp.where(mol == left, factor, 0.0)
        far = jnp.where(mol == right, 1.0, 0.0).astype(BF)
        high = mine.astype(BF)
        rest = mine - high.astype(F32)
        mid = rest.astype(BF)
        low = (rest - mid.astype(F32)).astype(BF)
        three = dot_nt(
            jnp.concatenate([high, mid, low], axis=0), jnp.concatenate([far, far], axis=0)
        )
        return three[:mols] + (three[mols : 2 * mols] + three[2 * mols :])

    for own, o in ((own_a, SELF), (own_r, TO_R), (own_u, TO_U), (own_c, TO_UR)):
        own[...] = weight(o)
    field = y.shape[1]
    for msg, o, q in (
        (msg_r, R_TO_A, R_TO_U),
        (msg_u, U_TO_A, U_TO_R),
        (msg_c, UR_TO_A, None),
    ):
        first = weight(o)
        if q is not None:
            lane = lax.broadcasted_iota(jnp.int32, first.shape, 1)
            first = jnp.where(lane < mols, first, weight(q))
        msg[:, :field] = y[...].astype(F32)
        msg[:, field : field + 2 * mols] = first
        msg[:, field + 2 * mols :] = jnp.concatenate(
            [e[...], jnp.zeros((mols, 2 * mols - e.shape[1]), F32)], axis=1
        )


def choose(core, low, high):
    return jnp.where(core[0, 0] == 1, high, low)


def self_body(states, rho, metric, own, proj, back, c_aa):
    rows = stack(rho, states)
    proj[...] = dot(rows, metric[...]).astype(BF)
    back[...] = dot_nt(rows, metric[...]).astype(BF)
    c_aa[...] = couple(proj[...], rows, own[...])


def first_body(states, core, rho, proj, back, own_u, own_c, msg_u, msg_c, c):
    mols = rho.shape[0]
    field = msg_u.shape[1] - 4 * mols
    part = slice(field, field + mols)
    rows = stack(rho, states)
    c[0] = couple(proj[...], rows, choose(core, own_u[...], own_c[...]))
    c[1] = couple(rows, back[...], twice(choose(core, msg_u[:, part], msg_c[:, part])))


def right_body(states, rho_a, rho_r, metric, proj_a, own, msg_r, proj_r, back_r, c):
    mols = rho_a.shape[0]
    field = msg_r.shape[1] - 4 * mols
    rows = stack(rho_r, states)
    proj_r[...] = dot(rows, metric[...]).astype(BF)
    back_r[...] = dot_nt(rows, metric[...]).astype(BF)
    c[0] = couple(proj_a[...], rows, own[...])
    c[1] = couple(proj_r[...], stack(rho_a, states), twice(msg_r[:, field : field + mols]))


def fields(states, core, y_a, msg_r, msg_u, msg_c):
    field = y_a.shape[1]
    f_a = stack(y_a, states)
    f_r, f_u, f_c = [stack(m[:, :field], states).astype(BF) for m in (msg_r, msg_u, msg_c)]
    return f_a, f_r, f_u, choose(core, f_u, f_c), choose(core, f_c, f_u)


def sums_of(core, c_aa, c_f, c_r, c_s, f_a, f_r, f_u, f_first, f_last):
    row_a = (dot(c_aa[...], f_a) + dot(c_f[0], f_first)) + (dot(c_r[0], f_r) + dot(c_s[0], f_last))
    row_r = dot(c_r[1], f_a) + dot(c_s[2], f_u)
    first, last = dot(c_f[1], f_a), dot(c_s[1], f_a)
    row_u = choose(core, first, last) + dot(c_s[3], f_r)
    return row_a, row_r, row_u, choose(core, last, first)


def corner_body(
    states,
    core,
    rho_f,
    near,
    shifted,
    proj_a,
    back_a,
    proj_r,
    back_r,
    own_u,
    own_c,
    msg_r,
    msg_u,
    msg_c,
    y_a,
    e_a,
    c_aa,
    c_f,
    c_r,
    c,
    to_a,
    to_r,
    to_uc,
    sums,
    rows,
):
    mols, field = y_a.shape
    width = rho_f.shape[1] // states
    part = slice(field, field + mols)
    half = slice(field + mols, field + 2 * mols)
    for a in range(states):
        lanes = slice(a * width, (a + 1) * width)
        place = slice(a * mols, (a + 1) * mols)
        rows[0, place] = rho_f[:, lanes]
        rows[1, place] = choose(core, near[:, lanes], shifted[:, lanes])
    upper = rows.at[core[0, 0]]
    last = rows[1]
    c[0] = couple(proj_a[...], last, choose(core, own_c[...], own_u[...]))
    c[1] = couple(last, back_a[...], twice(choose(core, msg_c[:, part], msg_u[:, part])))
    c[2] = couple(proj_r[...], upper[...], twice(msg_r[:, half]))
    c[3] = couple(upper[...], back_r[...], twice(msg_u[:, half]))
    f = fields(states, core, y_a, msg_r, msg_u, msg_c)
    row_a, row_r, row_u, row_c = sums_of(core, c_aa, c_f, c_r, c, *f)
    own_y = y_a[...].astype(F32)
    part_a = unstack(row_a, states) + spread(e_a[...], field // states) * own_y
    part_r, part_u, part_c = [unstack(row, states) for row in (row_r, row_u, row_c)]
    to_a[...], to_r[...], to_uc[0], to_uc[1] = part_a, part_r, part_u, part_c
    total = part_a * own_y + part_r * msg_r[:, :field]
    total = total + (part_u * msg_u[:, :field] + part_c * msg_c[:, :field])
    sums[0:1] = jnp.sum(total, axis=0, keepdims=True)
    sums[1:2] = jnp.sum(own_y * own_y, axis=0, keepdims=True)


def over_states(row, width):
    states = row.shape[1] // width
    total = row[:, :width]
    for a in range(1, states):
        total = total + row[:, a * width : (a + 1) * width]
    return jnp.concatenate([total] * states, axis=1)


def residual(sigma, y, e, theta, width):
    return (sigma - theta * y) / jnp.maximum(jnp.abs(spread(e, width) - theta), 1.0)


def theta_body(states, part, rest, sigma, y_a, e_a, theta, short, resid, squares):
    width = sigma.shape[1] // states
    sums = part[...] + rest[...]
    rate = over_states(sums[0:1], width) / over_states(sums[1:2], width)
    theta[...] = rate
    short[...] = rate[:, :width]
    value = residual(sigma[...], y_a[...].astype(F32), e_a[...], rate, width)
    resid[...] = value
    squares[...] = jnp.sum(value * value, axis=0, keepdims=True)


def second_body(
    states,
    core,
    theta,
    resid,
    sig_r,
    sig_uc,
    msg_r,
    msg_u,
    msg_c,
    c_aa,
    c_f,
    c_r,
    c_s,
    to_a,
    to_r,
    to_uc,
):
    mols, field = resid.shape
    width = field // states

    def other(sigma, msg):
        e = msg[:, field + 2 * mols : field + 2 * mols + states]
        value = residual(sigma, msg[:, :field], e, theta[...], width)
        return stack(value, states).astype(BF)

    f_a = stack(resid[...], states).astype(BF)
    f_r = other(sig_r[...], msg_r)
    f_u = other(sig_uc[0], msg_u)
    f_c = other(sig_uc[1], msg_c)
    rows = sums_of(
        core, c_aa, c_f, c_r, c_s, f_a, f_r, f_u, choose(core, f_u, f_c), choose(core, f_c, f_u)
    )
    to_a[...], to_r[...], to_uc[0], to_uc[1] = [unstack(row, states) for row in rows]


def last_body(states, count, part, rest, resid, to_a, below, left, e_a, corr, sigma):
    width = resid.shape[1] // states
    scale = jnp.sqrt(over_states(part[...] + rest[...], width) / count + 1e-06)
    value = (resid[...] / scale).astype(BF)
    corr[...] = value
    raw = (to_a[...] + below[0]) + left[...]
    sigma[...] = raw / scale + spread(e_a[...], width) * value.astype(F32)


def shards(densities, trials, energies, metric, pair_local, pair_remote, pair_scale):
    mols = densities.shape[2]
    states = energies.shape[3]
    aux = metric.shape[0]
    field = trials.shape[3]
    pairs = pair_local.shape[2]
    width = mols * states
    nx, ny = lax.axis_size("gx"), lax.axis_size("gy")

    def spot(x, y):
        return (x % nx) * ny + y % ny

    def take(value, dx, dy, only=lambda x, y: True):
        table = [
            (spot(x + dx, y + dy), spot(x, y))
            for x in range(nx)
            for y in range(ny)
            if only(x, y)
        ]
        return lax.ppermute(value, AXES, table)

    def along_z(table):
        def partner(x, y):
            z = table[(y // 2 % 2) * 4 + x % 4]
            return x // 4 * 4 + z % 4, y // 4 * 4 + z // 4 * 2 + y % 2

        return partner

    def flip(fx, fy):
        return lambda x, y: (x ^ fx, y ^ fy)

    steps = [
        along_z((3, 6, 5, 0, 7, 2, 1, 4)),
        along_z((7, 2, 1, 4, 3, 6, 5, 0)),
        along_z((1, 0, 3, 2, 5, 4, 7, 6)),
        flip(0, 4),
        flip(0, 12),
        flip(4, 0),
        flip(12, 0),
        flip(0, 1),
    ]

    def butterfly(value):
        for k, partner in enumerate(steps):
            table = [(spot(*partner(x, y)), spot(x, y)) for x in range(nx) for y in range(ny)]
            other = lax.ppermute(value, AXES, table)
            if k == len(steps) - 1:
                return value, other
            value = value + other

    rho_a, y_a, e_a = densities[0, 0], trials[0, 0], energies[0, 0]
    core = (lax.axis_index("gy") % 2).astype(jnp.int32).reshape(1, 1)
    table = [(spot(x + y % 2, y + 1), spot(x, y)) for x in range(nx) for y in range(ny)]
    rho_f = lax.ppermute(rho_a, AXES, table)

    pair = shape(mols, 2 * mols)
    note = shape(mols, field + 4 * mols)
    own_a, own_r, own_u, own_c, msg_r, msg_u, msg_c = call(
        functools.partial(weights_body, aux**-0.5),
        (pair, pair, pair, pair, note, note, note),
        9 * 2 * 3 * mols * 2 * mols * (pairs // 9),
        12 * pairs,
    )(pair_local[0], pair_remote[0], pair_scale[0], y_a, e_a)
    msg_r = take(msg_r, 1, 0)
    msg_u = take(msg_u, 0, 1)
    msg_c = take(msg_c, 1, 1)

    rho_r = take(rho_a, 1, 0)
    near = take(rho_r, 0, 1, lambda x, y: y % 2 == 0)
    shifted = take(rho_f, -1, 0, lambda x, y: y % 2 == 1)

    block = 2 * width * width * aux
    proj = 2 * width * aux * aux
    size = width * aux * 2
    wide, square = shape(width, aux, dtype=BF), shape(width, width, dtype=BF)
    squares_of = lambda count: shape(count, width, width, dtype=BF)
    proj_a, back_a, c_aa = call(
        functools.partial(self_body, states), (wide, wide, square), 2 * proj + block, 5 * size
    )(rho_a, metric, own_a)
    c_f = call(functools.partial(first_body, states), squares_of(2), 2 * block, 4 * size, 1)(
        core, rho_f, proj_a, back_a, own_u, own_c, msg_u, msg_c
    )
    proj_r, back_r, c_r = call(
        functools.partial(right_body, states),
        (wide, wide, squares_of(2)),
        2 * proj + 2 * block,
        8 * size,
    )(rho_a, rho_r, metric, proj_a, own_r, msg_r)
    one, two = shape(mols, field), shape(2, mols, field)
    c_s, to_a, to_r, to_uc, sums = call(
        functools.partial(corner_body, states),
        (squares_of(4), one, one, two, shape(2, field)),
        4 * block,
        9 * size,
        1,
        [pltpu.VMEM((2, width, aux), BF)],
    )(
        core,
        rho_f,
        near,
        shifted,
        proj_a,
        back_a,
        proj_r,
        back_r,
        own_u,
        own_c,
        msg_r,
        msg_u,
        msg_c,
        y_a,
        e_a,
        c_aa,
        c_f,
        c_r,
    )

    def home(to_r, to_uc):
        below = take(to_uc, 0, -1)
        left = take(to_r + below[1], -1, 0)
        return below, left

    sums = butterfly(sums)
    below, left = home(to_r, to_uc)
    sigma = (to_a + below[0]) + left
    sig_r = take(sigma, 1, 0)
    sig_uc = take(jnp.stack([sigma, sig_r]), 0, 1)
    theta, short, resid, squares = call(
        functools.partial(theta_body, states),
        (shape(1, field), shape(1, field // states), one, shape(1, field)),
        20 * mols * field,
        12 * mols * field,
    )(*sums, sigma, y_a, e_a)
    to_a, to_r, to_uc = call(
        functools.partial(second_body, states),
        (one, one, two),
        9 * 2 * width * field * mols,
        9 * width * width * 2,
        1,
    )(core, theta, resid, sig_r, sig_uc, msg_r, msg_u, msg_c, c_aa, c_f, c_r, c_s)
    squares = butterfly(squares)
    below, left = home(to_r, to_uc)
    corr, sigma2 = call(
        functools.partial(last_body, states, float(width * nx * ny)),
        (shape(mols, field, dtype=BF), one),
        20 * mols * field,
        16 * mols * field,
    )(*squares, resid, to_a, below, left, e_a)
    out = (1, 1, mols, field)
    return (
        sigma.reshape(out),
        corr.reshape(out),
        sigma2.reshape(out),
        short.reshape(field // states),
    )


def solution(mesh):
    return jax.shard_map(
        shards,
        mesh=mesh,
        in_specs=(
            P("gx", "gy", None, None),
            P("gx", "gy", None, None),
            P("gx", "gy", None, None),
            P(),
            P("gx", "gy", None),
            P("gx", "gy", None),
            P("gx", "gy", None),
        ),
        out_specs=(
            P("gx", "gy", None, None),
            P("gx", "gy", None, None),
            P("gx", "gy", None, None),
            P(),
        ),
        check_vma=False,
    )
```

```python
import functools

import jax
import jax.numpy as jnp
from jax import lax
from jax.experimental import pallas as pl
from jax.experimental.pallas import tpu as pltpu
from jax.sharding import PartitionSpec as P


BF = jnp.bfloat16
F32 = jnp.float32
AXES = ("gx", "gy")
SELF, TO_R, TO_U, TO_UR = 4, 7, 5, 8
R_TO_A, R_TO_U, U_TO_A, U_TO_R, UR_TO_A = 1, 2, 3, 6, 0


def vmem(count):
    return [pl.BlockSpec(memory_space=pltpu.VMEM)] * count


def call(body, outs, flops, moved, smem=0, scratch=()):
    return lambda *args: pl.pallas_call(
        body,
        out_shape=outs,
        in_specs=[pl.BlockSpec(memory_space=pltpu.SMEM)] * smem + vmem(len(args) - smem),
        out_specs=jax.tree.map(lambda _: pl.BlockSpec(memory_space=pltpu.VMEM), outs),
        scratch_shapes=scratch,
        compiler_params=pltpu.CompilerParams(vmem_limit_bytes=24 * 2**20),
        cost_estimate=pl.CostEstimate(flops=flops, bytes_accessed=moved, transcendentals=0),
    )(*args)


def shape(*dims, dtype=F32):
    return jax.ShapeDtypeStruct(dims, dtype)


def stack(ref, states):
    width = ref.shape[1] // states
    return jnp.concatenate([ref[:, a * width : (a + 1) * width] for a in range(states)], axis=0)


def unstack(value, states):
    mols = value.shape[0] // states
    return jnp.concatenate([value[a * mols : (a + 1) * mols] for a in range(states)], axis=1)


def dot_nt(a, b):
    return lax.dot_general(a, b, (((1,), (1,)), ((), ())), preferred_element_type=F32)


def dot(a, b):
    return jnp.dot(a, b, preferred_element_type=F32)


def twice(w):
    return jnp.concatenate([w, w], axis=1)


def couple(proj, rho, pair):
    dense = dot_nt(proj, rho)
    tiles = (dense.shape[0] // pair.shape[0], dense.shape[1] // pair.shape[1])
    return (dense * jnp.tile(pair, tiles)).astype(BF)


def spread(e, width):
    mols, states = e.shape
    lane = lax.broadcasted_iota(jnp.int32, (mols, states * width), 1) // width
    out = jnp.zeros((mols, states * width), F32)
    for a in range(states):
        out = jnp.where(lane == a, e[:, a : a + 1], out)
    return out


def weights_body(scale, loc, rem, sc, y, e, own_a, own_r, own_u, own_c, msg_r, msg_u, msg_c):
    mols = y.shape[0]
    cap = loc.shape[1] // 9
    mol = lax.broadcasted_iota(jnp.int32, (mols, cap), 0)

    def weight(o):
        part = slice(o * cap, (o + 1) * cap)
        left, right, factor = loc[:, part], rem[:, part], sc[:, part] * scale
        if o == 4:
            right = left + 1 + right
            right = jnp.where(right >= mols, right - mols, right)
        mine = jnp.where(mol == left, factor, 0.0)
        far = jnp.where(mol == right, 1.0, 0.0).astype(BF)
        high = mine.astype(BF)
        rest = mine - high.astype(F32)
        mid = rest.astype(BF)
        low = (rest - mid.astype(F32)).astype(BF)
        three = dot_nt(
            jnp.concatenate([high, mid, low], axis=0), jnp.concatenate([far, far], axis=0)
        )
        return three[:mols] + (three[mols : 2 * mols] + three[2 * mols :])

    for own, o in ((own_a, SELF), (own_r, TO_R), (own_u, TO_U), (own_c, TO_UR)):
        own[...] = weight(o)
    field = y.shape[1]
    for msg, o, q in (
        (msg_r, R_TO_A, R_TO_U),
        (msg_u, U_TO_A, U_TO_R),
        (msg_c, UR_TO_A, None),
    ):
        first = weight(o)
        if q is not None:
            lane = lax.broadcasted_iota(jnp.int32, first.shape, 1)
            first = jnp.where(lane < mols, first, weight(q))
        msg[:, :field] = y[...].astype(F32)
        msg[:, field : field + 2 * mols] = first
        msg[:, field + 2 * mols :] = jnp.concatenate(
            [e[...], jnp.zeros((mols, 2 * mols - e.shape[1]), F32)], axis=1
        )


def choose(core, low, high):
    return jnp.where(core[0, 0] == 1, high, low)


def self_body(states, rho, metric, own, proj, back, c_aa):
    rows = stack(rho, states)
    proj[...] = dot(rows, metric[...]).astype(BF)
    back[...] = dot_nt(rows, metric[...]).astype(BF)
    c_aa[...] = couple(proj[...], rows, own[...])


def stack_two(low, high, states):
    return jnp.concatenate([stack(low, states // 2), stack(high, states // 2)], axis=0)


def first_body(states, core, low, high, proj, back, own_u, own_c, msg_u, msg_c, c):
    mols = low.shape[0]
    field = msg_u.shape[1] - 4 * mols
    part = slice(field, field + mols)
    rows = stack_two(low, high, states)
    c[0] = couple(proj[...], rows, choose(core, own_u[...], own_c[...]))
    c[1] = couple(rows, back[...], twice(choose(core, msg_u[:, part], msg_c[:, part])))


def right_body(states, rho_a, low, high, metric, proj_a, own, msg_r, proj_r, back_r, c):
    mols = rho_a.shape[0]
    field = msg_r.shape[1] - 4 * mols
    rows = stack_two(low, high, states)
    proj_r[...] = dot(rows, metric[...]).astype(BF)
    back_r[...] = dot_nt(rows, metric[...]).astype(BF)
    c[0] = couple(proj_a[...], rows, own[...])
    c[1] = couple(proj_r[...], stack(rho_a, states), twice(msg_r[:, field : field + mols]))


def fields(states, core, y_a, msg_r, msg_u, msg_c):
    field = y_a.shape[1]
    f_a = stack(y_a, states)
    f_r, f_u, f_c = [stack(m[:, :field], states).astype(BF) for m in (msg_r, msg_u, msg_c)]
    return f_a, f_r, f_u, choose(core, f_u, f_c), choose(core, f_c, f_u)


def sums_of(core, c_aa, c_f, c_r, c_s, f_a, f_r, f_u, f_first, f_last):
    row_a = (dot(c_aa[...], f_a) + dot(c_f[0], f_first)) + (dot(c_r[0], f_r) + dot(c_s[0], f_last))
    row_r = dot(c_r[1], f_a) + dot(c_s[2], f_u)
    first, last = dot(c_f[1], f_a), dot(c_s[1], f_a)
    row_u = choose(core, first, last) + dot(c_s[3], f_r)
    return row_a, row_r, row_u, choose(core, last, first)


def corner_body(
    states,
    core,
    first_low,
    first_high,
    near_low,
    near_high,
    shift_low,
    shift_high,
    proj_a,
    back_a,
    proj_r,
    back_r,
    own_u,
    own_c,
    msg_r,
    msg_u,
    msg_c,
    y_a,
    e_a,
    c_aa,
    c_f,
    c_r,
    c,
    to_a,
    to_r,
    to_uc,
    sums,
    rows,
):
    mols, field = y_a.shape
    width = first_low.shape[1] * 2 // states
    part = slice(field, field + mols)
    half = slice(field + mols, field + 2 * mols)
    halves = ((first_low, near_low, shift_low), (first_high, near_high, shift_high))
    for a in range(states):
        first, near, shifted = halves[a * 2 // states]
        b = a % (states // 2)
        lanes = slice(b * width, (b + 1) * width)
        place = slice(a * mols, (a + 1) * mols)
        rows[0, place] = first[:, lanes]
        rows[1, place] = choose(core, near[:, lanes], shifted[:, lanes])
    upper = rows.at[core[0, 0]]
    last = rows[1]
    c[0] = couple(proj_a[...], last, choose(core, own_c[...], own_u[...]))
    c[1] = couple(last, back_a[...], twice(choose(core, msg_c[:, part], msg_u[:, part])))
    c[2] = couple(proj_r[...], upper[...], twice(msg_r[:, half]))
    c[3] = couple(upper[...], back_r[...], twice(msg_u[:, half]))
    f = fields(states, core, y_a, msg_r, msg_u, msg_c)
    row_a, row_r, row_u, row_c = sums_of(core, c_aa, c_f, c_r, c, *f)
    own_y = y_a[...].astype(F32)
    part_a = unstack(row_a, states) + spread(e_a[...], field // states) * own_y
    part_r, part_u, part_c = [unstack(row, states) for row in (row_r, row_u, row_c)]
    to_a[...], to_r[...], to_uc[0], to_uc[1] = part_a, part_r, part_u, part_c
    total = part_a * own_y + part_r * msg_r[:, :field]
    total = total + (part_u * msg_u[:, :field] + part_c * msg_c[:, :field])
    sums[0:1] = jnp.sum(total, axis=0, keepdims=True)
    sums[1:2] = jnp.sum(own_y * own_y, axis=0, keepdims=True)


def over_states(row, width):
    states = row.shape[1] // width
    total = row[:, :width]
    for a in range(1, states):
        total = total + row[:, a * width : (a + 1) * width]
    return jnp.concatenate([total] * states, axis=1)


def residual(sigma, y, e, theta, width):
    return (sigma - theta * y) / jnp.maximum(jnp.abs(spread(e, width) - theta), 1.0)


def theta_body(states, part, rest, sigma, y_a, e_a, theta, short, resid, squares):
    width = sigma.shape[1] // states
    sums = part[...] + rest[...]
    rate = over_states(sums[0:1], width) / over_states(sums[1:2], width)
    theta[...] = rate
    short[...] = rate[:, :width]
    value = residual(sigma[...], y_a[...].astype(F32), e_a[...], rate, width)
    resid[...] = value
    squares[...] = jnp.sum(value * value, axis=0, keepdims=True)


def second_body(
    states,
    core,
    theta,
    resid,
    sig_r,
    sig_uc,
    msg_r,
    msg_u,
    msg_c,
    c_aa,
    c_f,
    c_r,
    c_s,
    to_a,
    to_r,
    to_uc,
):
    mols, field = resid.shape
    width = field // states

    def other(sigma, msg):
        e = msg[:, field + 2 * mols : field + 2 * mols + states]
        value = residual(sigma, msg[:, :field], e, theta[...], width)
        return stack(value, states).astype(BF)

    f_a = stack(resid[...], states).astype(BF)
    f_r = other(sig_r[...], msg_r)
    f_u = other(sig_uc[0], msg_u)
    f_c = other(sig_uc[1], msg_c)
    rows = sums_of(
        core, c_aa, c_f, c_r, c_s, f_a, f_r, f_u, choose(core, f_u, f_c), choose(core, f_c, f_u)
    )
    to_a[...], to_r[...], to_uc[0], to_uc[1] = [unstack(row, states) for row in rows]


def last_body(states, count, part, rest, resid, to_a, below, left, e_a, corr, sigma):
    width = resid.shape[1] // states
    scale = jnp.sqrt(over_states(part[...] + rest[...], width) / count + 1e-06)
    value = (resid[...] / scale).astype(BF)
    corr[...] = value
    raw = (to_a[...] + below[0]) + left[...]
    sigma[...] = raw / scale + spread(e_a[...], width) * value.astype(F32)


def shards(densities, trials, energies, metric, pair_local, pair_remote, pair_scale):
    mols = densities.shape[2]
    states = energies.shape[3]
    aux = metric.shape[0]
    field = trials.shape[3]
    pairs = pair_local.shape[2]
    width = mols * states
    nx, ny = lax.axis_size("gx"), lax.axis_size("gy")

    def spot(x, y):
        return (x % nx) * ny + y % ny

    def take(value, dx, dy, only=lambda x, y: True):
        table = [
            (spot(x + dx, y + dy), spot(x, y))
            for x in range(nx)
            for y in range(ny)
            if only(x, y)
        ]
        return lax.ppermute(value, AXES, table)

    def along_z(table):
        def partner(x, y):
            z = table[(y // 2 % 2) * 4 + x % 4]
            return x // 4 * 4 + z % 4, y // 4 * 4 + z // 4 * 2 + y % 2

        return partner

    def flip(fx, fy):
        return lambda x, y: (x ^ fx, y ^ fy)

    steps = [
        along_z((3, 6, 5, 0, 7, 2, 1, 4)),
        along_z((7, 2, 1, 4, 3, 6, 5, 0)),
        along_z((1, 0, 3, 2, 5, 4, 7, 6)),
        flip(0, 4),
        flip(0, 12),
        flip(4, 0),
        flip(12, 0),
        flip(0, 1),
    ]

    def butterfly(value, steps):
        for k, partner in enumerate(steps):
            table = [(spot(*partner(x, y)), spot(x, y)) for x in range(nx) for y in range(ny)]
            other = lax.ppermute(value, AXES, table)
            if k == len(steps) - 1:
                return value, other
            value = value + other

    rho_a, y_a, e_a = densities[0, 0], trials[0, 0], energies[0, 0]
    core = (lax.axis_index("gy") % 2).astype(jnp.int32).reshape(1, 1)
    table = [(spot(x + y % 2, y + 1), spot(x, y)) for x in range(nx) for y in range(ny)]
    half = rho_a.shape[1] // 2
    first_low = lax.ppermute(rho_a[:, :half], AXES, table)
    first_high = lax.ppermute(rho_a[:, half:], AXES, table)
    right_low = take(rho_a[:, :half], 1, 0)
    right_high = take(rho_a[:, half:], 1, 0)

    pair = shape(mols, 2 * mols)
    note = shape(mols, field + 4 * mols)
    own_a, own_r, own_u, own_c, msg_r, msg_u, msg_c = call(
        functools.partial(weights_body, aux**-0.5),
        (pair, pair, pair, pair, note, note, note),
        9 * 2 * 3 * mols * 2 * mols * (pairs // 9),
        12 * pairs,
    )(pair_local[0], pair_remote[0], pair_scale[0], y_a, e_a)
    msg_r = take(msg_r, 1, 0)
    msg_u = take(msg_u, 0, 1)
    msg_c = take(msg_c, 1, 1)

    even, odd = (lambda x, y: y % 2 == 0), (lambda x, y: y % 2 == 1)
    shift_low = take(first_low, -1, 0, odd)
    shift_high = take(first_high, -1, 0, odd)
    near_low = take(right_low, 0, 1, even)
    near_high = take(right_high, 0, 1, even)

    block = 2 * width * width * aux
    proj = 2 * width * aux * aux
    size = width * aux * 2
    wide, square = shape(width, aux, dtype=BF), shape(width, width, dtype=BF)
    squares_of = lambda count: shape(count, width, width, dtype=BF)
    proj_a, back_a, c_aa = call(
        functools.partial(self_body, states), (wide, wide, square), 2 * proj + block, 5 * size
    )(rho_a, metric, own_a)
    c_f = call(functools.partial(first_body, states), squares_of(2), 2 * block, 4 * size, 1)(
        core, first_low, first_high, proj_a, back_a, own_u, own_c, msg_u, msg_c
    )
    proj_r, back_r, c_r = call(
        functools.partial(right_body, states),
        (wide, wide, squares_of(2)),
        2 * proj + 2 * block,
        8 * size,
    )(rho_a, right_low, right_high, metric, proj_a, own_r, msg_r)
    one, two = shape(mols, field), shape(2, mols, field)
    c_s, to_a, to_r, to_uc, sums = call(
        functools.partial(corner_body, states),
        (squares_of(4), one, one, two, shape(2, field)),
        4 * block,
        9 * size,
        1,
        [pltpu.VMEM((2, width, aux), BF)],
    )(
        core,
        first_low,
        first_high,
        near_low,
        near_high,
        shift_low,
        shift_high,
        proj_a,
        back_a,
        proj_r,
        back_r,
        own_u,
        own_c,
        msg_r,
        msg_u,
        msg_c,
        y_a,
        e_a,
        c_aa,
        c_f,
        c_r,
    )

    def home(to_r, to_uc):
        below = take(to_uc, 0, -1)
        left = take(to_r + below[1], -1, 0)
        return below, left

    sums = butterfly(sums, steps)
    below, left = home(to_r, to_uc)
    sigma = (to_a + below[0]) + left
    sig_r = take(sigma, 1, 0)
    sig_uc = take(jnp.stack([sigma, sig_r]), 0, 1)
    theta, short, resid, squares = call(
        functools.partial(theta_body, states),
        (shape(1, field), shape(1, field // states), one, shape(1, field)),
        20 * mols * field,
        12 * mols * field,
    )(*sums, sigma, y_a, e_a)
    to_a, to_r, to_uc = call(
        functools.partial(second_body, states),
        (one, one, two),
        9 * 2 * width * field * mols,
        9 * width * width * 2,
        1,
    )(core, theta, resid, sig_r, sig_uc, msg_r, msg_u, msg_c, c_aa, c_f, c_r, c_s)
    squares = butterfly(squares, [steps[3], *steps[:3], *steps[4:]])
    below, left = home(to_r, to_uc)
    corr, sigma2 = call(
        functools.partial(last_body, states, float(width * nx * ny)),
        (shape(mols, field, dtype=BF), one),
        20 * mols * field,
        16 * mols * field,
    )(*squares, resid, to_a, below, left, e_a)
    out = (1, 1, mols, field)
    return (
        sigma.reshape(out),
        corr.reshape(out),
        sigma2.reshape(out),
        short.reshape(field // states),
    )


def solution(mesh):
    return jax.shard_map(
        shards,
        mesh=mesh,
        in_specs=(
            P("gx", "gy", None, None),
            P("gx", "gy", None, None),
            P("gx", "gy", None, None),
            P(),
            P("gx", "gy", None),
            P("gx", "gy", None),
            P("gx", "gy", None),
        ),
        out_specs=(
            P("gx", "gy", None, None),
            P("gx", "gy", None, None),
            P("gx", "gy", None, None),
            P(),
        ),
        check_vma=False,
    )
```

```python
import functools

import jax
import jax.numpy as jnp
from jax import lax
from jax.experimental import pallas as pl
from jax.experimental.pallas import tpu as pltpu
from jax.sharding import PartitionSpec as P


BF = jnp.bfloat16
F32 = jnp.float32
AXES = ("gx", "gy")
SELF, TO_R, TO_U, TO_UR = 4, 7, 5, 8
R_TO_A, R_TO_U, U_TO_A, U_TO_R, UR_TO_A = 1, 2, 3, 6, 0


def vmem(count):
    return [pl.BlockSpec(memory_space=pltpu.VMEM)] * count


def call(body, outs, flops, moved, smem=0, scratch=()):
    return lambda *args: pl.pallas_call(
        body,
        out_shape=outs,
        in_specs=[pl.BlockSpec(memory_space=pltpu.SMEM)] * smem + vmem(len(args) - smem),
        out_specs=jax.tree.map(lambda _: pl.BlockSpec(memory_space=pltpu.VMEM), outs),
        scratch_shapes=scratch,
        compiler_params=pltpu.CompilerParams(vmem_limit_bytes=24 * 2**20),
        cost_estimate=pl.CostEstimate(flops=flops, bytes_accessed=moved, transcendentals=0),
    )(*args)


def shape(*dims, dtype=F32):
    return jax.ShapeDtypeStruct(dims, dtype)


def stack(ref, states):
    width = ref.shape[1] // states
    return jnp.concatenate([ref[:, a * width : (a + 1) * width] for a in range(states)], axis=0)


def unstack(value, states):
    mols = value.shape[0] // states
    return jnp.concatenate([value[a * mols : (a + 1) * mols] for a in range(states)], axis=1)


def dot_nt(a, b):
    return lax.dot_general(a, b, (((1,), (1,)), ((), ())), preferred_element_type=F32)


def dot(a, b):
    return jnp.dot(a, b, preferred_element_type=F32)


def twice(w):
    return jnp.concatenate([w, w], axis=1)


def couple(proj, rho, pair):
    dense = dot_nt(proj, rho)
    tiles = (dense.shape[0] // pair.shape[0], dense.shape[1] // pair.shape[1])
    return (dense * jnp.tile(pair, tiles)).astype(BF)


def spread(e, width):
    mols, states = e.shape
    lane = lax.broadcasted_iota(jnp.int32, (mols, states * width), 1) // width
    out = jnp.zeros((mols, states * width), F32)
    for a in range(states):
        out = jnp.where(lane == a, e[:, a : a + 1], out)
    return out


def weights_body(scale, loc, rem, sc, y, e, own_a, own_r, own_u, own_c, msg_r, msg_u, msg_c):
    mols = y.shape[0]
    cap = loc.shape[1] // 9
    mol = lax.broadcasted_iota(jnp.int32, (mols, cap), 0)

    def weight(o):
        part = slice(o * cap, (o + 1) * cap)
        left, right, factor = loc[:, part], rem[:, part], sc[:, part] * scale
        if o == 4:
            right = left + 1 + right
            right = jnp.where(right >= mols, right - mols, right)
        mine = jnp.where(mol == left, factor, 0.0)
        far = jnp.where(mol == right, 1.0, 0.0).astype(BF)
        three = dot_nt(
            jnp.concatenate(split(mine, 3), axis=0), jnp.concatenate([far, far], axis=0)
        )
        return three[:mols] + (three[mols : 2 * mols] + three[2 * mols :])

    for own, o in ((own_a, SELF), (own_r, TO_R), (own_u, TO_U), (own_c, TO_UR)):
        own[...] = weight(o)
    for msg, o, q in (
        (msg_r, R_TO_A, R_TO_U),
        (msg_u, U_TO_A, U_TO_R),
        (msg_c, UR_TO_A, None),
    ):
        first = weight(o)
        if q is not None:
            lane = lax.broadcasted_iota(jnp.int32, first.shape, 1)
            first = jnp.where(lane < mols, first, weight(q))
        energies = split(e[...], 3)
        used = 3 * e.shape[1]
        parts = [y[...], *split(first, 2), *energies, jnp.zeros((mols, 2 * mols - used), BF)]
        msg[...] = jnp.concatenate(parts, axis=1)


def choose(core, low, high):
    return jnp.where(core[0, 0] == 1, high, low)


def self_body(states, rho, metric, own, proj, back, c_aa):
    rows = stack(rho, states)
    proj[...] = dot(rows, metric[...]).astype(BF)
    back[...] = dot_nt(rows, metric[...]).astype(BF)
    c_aa[...] = couple(proj[...], rows, own[...])


def stack_two(low, high, states):
    return jnp.concatenate([stack(low, states // 2), stack(high, states // 2)], axis=0)


def note_weights(note, mols, k):
    base = note.shape[1] - 6 * mols + k * mols
    high, low = note[:, base : base + mols], note[:, base + 2 * mols : base + 3 * mols]
    return high.astype(F32) + low.astype(F32)


def note_energies(note, states):
    base = note.shape[1] - 2 * note.shape[0]
    parts = [note[:, base + k * states : base + (k + 1) * states].astype(F32) for k in range(3)]
    return parts[0] + (parts[1] + parts[2])


def split(value, count):
    parts = []
    for _ in range(count):
        parts.append(value.astype(BF))
        value = value - parts[-1].astype(F32)
    return parts


def first_body(states, core, rho, proj, back, own_u, own_c, msg_u, msg_c, c):
    mols = rho.shape[0]
    rows = stack(rho, states)
    c[0] = couple(proj[...], rows, choose(core, own_u[...], own_c[...]))
    pair = choose(core, note_weights(msg_u, mols, 0), note_weights(msg_c, mols, 0))
    c[1] = couple(rows, back[...], twice(pair))


def right_body(states, rho_a, low, high, metric, proj_a, own, msg_r, proj_r, back_r, c):
    mols = rho_a.shape[0]
    rows = stack_two(low, high, states)
    proj_r[...] = dot(rows, metric[...]).astype(BF)
    back_r[...] = dot_nt(rows, metric[...]).astype(BF)
    c[0] = couple(proj_a[...], rows, own[...])
    c[1] = couple(proj_r[...], stack(rho_a, states), twice(note_weights(msg_r, mols, 0)))


def fields(states, core, y_a, msg_r, msg_u, msg_c):
    field = y_a.shape[1]
    f_a = stack(y_a, states)
    f_r, f_u, f_c = [stack(m[:, :field], states) for m in (msg_r, msg_u, msg_c)]
    return f_a, f_r, f_u, choose(core, f_u, f_c), choose(core, f_c, f_u)


def sums_of(core, c_aa, c_f, c_r, c_s, f_a, f_r, f_u, f_first, f_last):
    row_a = (dot(c_aa[...], f_a) + dot(c_f[0], f_first)) + (dot(c_r[0], f_r) + dot(c_s[0], f_last))
    row_r = dot(c_r[1], f_a) + dot(c_s[2], f_u)
    first, last = dot(c_f[1], f_a), dot(c_s[1], f_a)
    row_u = choose(core, first, last) + dot(c_s[3], f_r)
    return row_a, row_r, row_u, choose(core, last, first)


def corner_body(
    states,
    core,
    rho_f,
    near_low,
    near_high,
    shifted,
    proj_a,
    back_a,
    proj_r,
    back_r,
    own_u,
    own_c,
    msg_r,
    msg_u,
    msg_c,
    y_a,
    e_a,
    c_aa,
    c_f,
    c_r,
    c,
    to_a,
    to_r,
    to_uc,
    sums,
    rows,
):
    mols, field = y_a.shape
    width = rho_f.shape[1] // states
    for a in range(states):
        near = (near_low, near_high)[a * 2 // states]
        b = a % (states // 2)
        lanes = slice(a * width, (a + 1) * width)
        place = slice(a * mols, (a + 1) * mols)
        rows[0, place] = rho_f[:, lanes]
        rows[1, place] = choose(core, near[:, b * width : (b + 1) * width], shifted[:, lanes])
    upper = rows.at[core[0, 0]]
    last = rows[1]
    c[0] = couple(proj_a[...], last, choose(core, own_c[...], own_u[...]))
    pair = choose(core, note_weights(msg_c, mols, 0), note_weights(msg_u, mols, 0))
    c[1] = couple(last, back_a[...], twice(pair))
    c[2] = couple(proj_r[...], upper[...], twice(note_weights(msg_r, mols, 1)))
    c[3] = couple(upper[...], back_r[...], twice(note_weights(msg_u, mols, 1)))
    f = fields(states, core, y_a, msg_r, msg_u, msg_c)
    row_a, row_r, row_u, row_c = sums_of(core, c_aa, c_f, c_r, c, *f)
    own_y = y_a[...].astype(F32)
    part_a = unstack(row_a, states) + spread(e_a[...], field // states) * own_y
    part_r, part_u, part_c = [unstack(row, states) for row in (row_r, row_u, row_c)]
    to_a[...], to_r[...], to_uc[0], to_uc[1] = part_a, part_r, part_u, part_c
    y_r, y_u, y_c = [m[:, :field].astype(F32) for m in (msg_r, msg_u, msg_c)]
    total = (part_a * own_y + part_r * y_r) + (part_u * y_u + part_c * y_c)
    sums[0:1] = jnp.sum(total, axis=0, keepdims=True)
    sums[1:2] = jnp.sum(own_y * own_y, axis=0, keepdims=True)


def over_states(row, width):
    states = row.shape[1] // width
    total = row[:, :width]
    for a in range(1, states):
        total = total + row[:, a * width : (a + 1) * width]
    return jnp.concatenate([total] * states, axis=1)


def residual(sigma, y, e, theta, width):
    return (sigma - theta * y) / jnp.maximum(jnp.abs(spread(e, width) - theta), 1.0)


def theta_body(states, part, rest, sigma, y_a, e_a, theta, short, resid, squares):
    width = sigma.shape[1] // states
    sums = part[...] + rest[...]
    rate = over_states(sums[0:1], width) / over_states(sums[1:2], width)
    theta[...] = rate
    short[...] = rate[:, :width]
    value = residual(sigma[...], y_a[...].astype(F32), e_a[...], rate, width)
    resid[...] = value
    squares[...] = jnp.sum(value * value, axis=0, keepdims=True)


def second_body(
    states,
    core,
    theta,
    resid,
    sig_r,
    sig_uc,
    msg_r,
    msg_u,
    msg_c,
    c_aa,
    c_f,
    c_r,
    c_s,
    to_a,
    to_r,
    to_uc,
):
    _, field = resid.shape
    width = field // states

    def other(sigma, msg):
        e = note_energies(msg, states)
        value = residual(sigma, msg[:, :field].astype(F32), e, theta[...], width)
        return stack(value, states).astype(BF)

    f_a = stack(resid[...], states).astype(BF)
    f_r = other(sig_r[...], msg_r)
    f_u = other(sig_uc[0], msg_u)
    f_c = other(sig_uc[1], msg_c)
    rows = sums_of(
        core, c_aa, c_f, c_r, c_s, f_a, f_r, f_u, choose(core, f_u, f_c), choose(core, f_c, f_u)
    )
    to_a[...], to_r[...], to_uc[0], to_uc[1] = [unstack(row, states) for row in rows]


def last_body(states, count, part, rest, resid, to_a, below, left, e_a, corr, sigma):
    width = resid.shape[1] // states
    scale = jnp.sqrt(over_states(part[...] + rest[...], width) / count + 1e-06)
    value = (resid[...] / scale).astype(BF)
    corr[...] = value
    raw = (to_a[...] + below[0]) + left[...]
    sigma[...] = raw / scale + spread(e_a[...], width) * value.astype(F32)


def shards(densities, trials, energies, metric, pair_local, pair_remote, pair_scale):
    mols = densities.shape[2]
    states = energies.shape[3]
    aux = metric.shape[0]
    field = trials.shape[3]
    pairs = pair_local.shape[2]
    width = mols * states
    nx, ny = lax.axis_size("gx"), lax.axis_size("gy")

    def spot(x, y):
        return (x % nx) * ny + y % ny

    def take(value, dx, dy, only=lambda x, y: True):
        table = [
            (spot(x + dx, y + dy), spot(x, y))
            for x in range(nx)
            for y in range(ny)
            if only(x, y)
        ]
        return lax.ppermute(value, AXES, table)

    def along_z(table):
        def partner(x, y):
            z = table[(y // 2 % 2) * 4 + x % 4]
            return x // 4 * 4 + z % 4, y // 4 * 4 + z // 4 * 2 + y % 2

        return partner

    def flip(fx, fy):
        return lambda x, y: (x ^ fx, y ^ fy)

    steps = [
        along_z((3, 6, 5, 0, 7, 2, 1, 4)),
        along_z((7, 2, 1, 4, 3, 6, 5, 0)),
        along_z((1, 0, 3, 2, 5, 4, 7, 6)),
        flip(0, 4),
        flip(0, 12),
        flip(4, 0),
        flip(12, 0),
        flip(0, 1),
    ]
    z_far, z_mid, z_near, x_near, x_far, y_near, y_far, chip = steps

    def butterfly(value, steps):
        for k, partner in enumerate(steps):
            table = [(spot(*partner(x, y)), spot(x, y)) for x in range(nx) for y in range(ny)]
            other = lax.ppermute(value, AXES, table)
            if k == len(steps) - 1:
                return value, other
            value = value + other

    rho_a, y_a, e_a = densities[0, 0], trials[0, 0], energies[0, 0]
    core = (lax.axis_index("gy") % 2).astype(jnp.int32).reshape(1, 1)
    table = [(spot(x + y % 2, y + 1), spot(x, y)) for x in range(nx) for y in range(ny)]
    rho_f = lax.ppermute(rho_a, AXES, table)

    pair = shape(mols, 2 * mols)
    note = shape(mols, field + 6 * mols, dtype=BF)
    own_a, own_r, own_u, own_c, msg_r, msg_u, msg_c = call(
        functools.partial(weights_body, aux**-0.5),
        (pair, pair, pair, pair, note, note, note),
        9 * 2 * 3 * mols * 2 * mols * (pairs // 9),
        12 * pairs,
    )(pair_local[0], pair_remote[0], pair_scale[0], y_a, e_a)
    msg_r = take(msg_r, 1, 0)
    msg_u = take(msg_u, 0, 1)
    msg_c = take(msg_c, 1, 1)

    half = rho_a.shape[1] // 2
    even, odd = (lambda x, y: y % 2 == 0), (lambda x, y: y % 2 == 1)
    right_low = take(rho_a[:, :half], 1, 0)
    right_high = take(rho_a[:, half:], 1, 0)
    shifted = take(rho_f, -1, 0, odd)
    near_low = take(right_low, 0, 1, even)
    near_high = take(right_high, 0, 1, even)

    block = 2 * width * width * aux
    proj = 2 * width * aux * aux
    size = width * aux * 2
    wide, square = shape(width, aux, dtype=BF), shape(width, width, dtype=BF)
    squares_of = lambda count: shape(count, width, width, dtype=BF)
    proj_a, back_a, c_aa = call(
        functools.partial(self_body, states), (wide, wide, square), 2 * proj + block, 5 * size
    )(rho_a, metric, own_a)
    c_f = call(functools.partial(first_body, states), squares_of(2), 2 * block, 4 * size, 1)(
        core, rho_f, proj_a, back_a, own_u, own_c, msg_u, msg_c
    )
    proj_r, back_r, c_r = call(
        functools.partial(right_body, states),
        (wide, wide, squares_of(2)),
        2 * proj + 2 * block,
        8 * size,
    )(rho_a, right_low, right_high, metric, proj_a, own_r, msg_r)
    one, two = shape(mols, field), shape(2, mols, field)
    c_s, to_a, to_r, to_uc, sums = call(
        functools.partial(corner_body, states),
        (squares_of(4), one, one, two, shape(2, field)),
        4 * block,
        9 * size,
        1,
        [pltpu.VMEM((2, width, aux), BF)],
    )(
        core,
        rho_f,
        near_low,
        near_high,
        shifted,
        proj_a,
        back_a,
        proj_r,
        back_r,
        own_u,
        own_c,
        msg_r,
        msg_u,
        msg_c,
        y_a,
        e_a,
        c_aa,
        c_f,
        c_r,
    )

    def home(to_r, to_uc):
        below = take(to_uc, 0, -1)
        left = take(to_r + below[1], -1, 0)
        return below, left

    sums = butterfly(sums, [z_far, chip, z_mid, z_near, x_near, x_far, y_near, y_far])
    below, left = home(to_r, to_uc)
    sigma = (to_a + below[0]) + left
    sig_r = take(sigma, 1, 0)
    sig_uc = take(jnp.stack([sigma, sig_r]), 0, 1)
    theta, short, resid, squares = call(
        functools.partial(theta_body, states),
        (shape(1, field), shape(1, field // states), one, shape(1, field)),
        20 * mols * field,
        12 * mols * field,
    )(*sums, sigma, y_a, e_a)
    to_a, to_r, to_uc = call(
        functools.partial(second_body, states),
        (one, one, two),
        9 * 2 * width * field * mols,
        9 * width * width * 2,
        1,
    )(core, theta, resid, sig_r, sig_uc, msg_r, msg_u, msg_c, c_aa, c_f, c_r, c_s)
    squares = butterfly(squares, [x_near, z_far, chip, z_mid, z_near, x_far, y_near, y_far])
    below, left = home(to_r, to_uc)
    corr, sigma2 = call(
        functools.partial(last_body, states, float(width * nx * ny)),
        (shape(mols, field, dtype=BF), one),
        20 * mols * field,
        16 * mols * field,
    )(*squares, resid, to_a, below, left, e_a)
    out = (1, 1, mols, field)
    return (
        sigma.reshape(out),
        corr.reshape(out),
        sigma2.reshape(out),
        short.reshape(field // states),
    )


def solution(mesh):
    return jax.shard_map(
        shards,
        mesh=mesh,
        in_specs=(
            P("gx", "gy", None, None),
            P("gx", "gy", None, None),
            P("gx", "gy", None, None),
            P(),
            P("gx", "gy", None),
            P("gx", "gy", None),
            P("gx", "gy", None),
        ),
        out_specs=(
            P("gx", "gy", None, None),
            P("gx", "gy", None, None),
            P("gx", "gy", None, None),
            P(),
        ),
        check_vma=False,
    )
```

```python
import functools

import jax
import jax.numpy as jnp
from jax import lax
from jax.experimental import pallas as pl
from jax.experimental.pallas import tpu as pltpu
from jax.sharding import PartitionSpec as P


BF = jnp.bfloat16
F32 = jnp.float32
AXES = ("gx", "gy")
SELF, TO_R, TO_U, TO_UR = 4, 7, 5, 8
R_TO_A, R_TO_U, U_TO_A, U_TO_R, UR_TO_A = 1, 2, 3, 6, 0


def vmem(count):
    return [pl.BlockSpec(memory_space=pltpu.VMEM)] * count


def call(body, outs, flops, moved, smem=0, scratch=()):
    return lambda *args: pl.pallas_call(
        body,
        out_shape=outs,
        in_specs=[pl.BlockSpec(memory_space=pltpu.SMEM)] * smem + vmem(len(args) - smem),
        out_specs=jax.tree.map(lambda _: pl.BlockSpec(memory_space=pltpu.VMEM), outs),
        scratch_shapes=scratch,
        compiler_params=pltpu.CompilerParams(vmem_limit_bytes=24 * 2**20),
        cost_estimate=pl.CostEstimate(flops=flops, bytes_accessed=moved, transcendentals=0),
    )(*args)


def shape(*dims, dtype=F32):
    return jax.ShapeDtypeStruct(dims, dtype)


def stack(ref, states):
    width = ref.shape[1] // states
    return jnp.concatenate([ref[:, a * width : (a + 1) * width] for a in range(states)], axis=0)


def unstack(value, states):
    mols = value.shape[0] // states
    return jnp.concatenate([value[a * mols : (a + 1) * mols] for a in range(states)], axis=1)


def dot_nt(a, b):
    return lax.dot_general(a, b, (((1,), (1,)), ((), ())), preferred_element_type=F32)


def dot(a, b):
    return jnp.dot(a, b, preferred_element_type=F32)


def twice(w):
    return jnp.concatenate([w, w], axis=1)


def couple(proj, rho, pair):
    dense = dot_nt(proj, rho)
    tiles = (dense.shape[0] // pair.shape[0], dense.shape[1] // pair.shape[1])
    return (dense * jnp.tile(pair, tiles)).astype(BF)


def spread(e, width):
    mols, states = e.shape
    lane = lax.broadcasted_iota(jnp.int32, (mols, states * width), 1) // width
    out = jnp.zeros((mols, states * width), F32)
    for a in range(states):
        out = jnp.where(lane == a, e[:, a : a + 1], out)
    return out


def weights_body(scale, loc, rem, sc, y, e, own_a, own_r, own_u, own_c, msg_r, msg_u, msg_c):
    mols = y.shape[0]
    cap = loc.shape[1] // 9
    mol = lax.broadcasted_iota(jnp.int32, (mols, cap), 0)

    def weight(o):
        part = slice(o * cap, (o + 1) * cap)
        left, right, factor = loc[:, part], rem[:, part], sc[:, part] * scale
        if o == 4:
            right = left + 1 + right
            right = jnp.where(right >= mols, right - mols, right)
        mine = jnp.where(mol == left, factor, 0.0)
        far = jnp.where(mol == right, 1.0, 0.0).astype(BF)
        three = dot_nt(
            jnp.concatenate(split(mine, 3), axis=0), jnp.concatenate([far, far], axis=0)
        )
        return three[:mols] + (three[mols : 2 * mols] + three[2 * mols :])

    for own, o in ((own_a, SELF), (own_r, TO_R), (own_u, TO_U), (own_c, TO_UR)):
        own[...] = weight(o)
    for msg, o, q in (
        (msg_r, R_TO_A, R_TO_U),
        (msg_u, U_TO_A, U_TO_R),
        (msg_c, UR_TO_A, None),
    ):
        first = weight(o)
        if q is not None:
            lane = lax.broadcasted_iota(jnp.int32, first.shape, 1)
            first = jnp.where(lane < mols, first, weight(q))
        energies = split(e[...], 3)
        used = 3 * e.shape[1]
        parts = [y[...], *split(first, 2), *energies, jnp.zeros((mols, 2 * mols - used), BF)]
        msg[...] = jnp.concatenate(parts, axis=1)


def choose(core, low, high):
    return jnp.where(core[0, 0] == 1, high, low)


def self_body(states, rho, metric, own, proj, back, c_aa):
    rows = stack(rho, states)
    proj[...] = dot(rows, metric[...]).astype(BF)
    back[...] = dot_nt(rows, metric[...]).astype(BF)
    c_aa[...] = couple(proj[...], rows, own[...])


def stack_two(low, high, states):
    return jnp.concatenate([stack(low, states // 2), stack(high, states // 2)], axis=0)


def note_weights(note, mols, k):
    base = note.shape[1] - 6 * mols + k * mols
    high, low = note[:, base : base + mols], note[:, base + 2 * mols : base + 3 * mols]
    return high.astype(F32) + low.astype(F32)


def note_energies(note, states):
    base = note.shape[1] - 2 * note.shape[0]
    parts = [note[:, base + k * states : base + (k + 1) * states].astype(F32) for k in range(3)]
    return parts[0] + (parts[1] + parts[2])


def split(value, count):
    parts = []
    for _ in range(count):
        parts.append(value.astype(BF))
        value = value - parts[-1].astype(F32)
    return parts


def first_body(states, core, low, high, proj, back, own_u, own_c, msg_u, msg_c, c):
    mols = low.shape[0]
    rows = stack_two(low, high, states)
    c[0] = couple(proj[...], rows, choose(core, own_u[...], own_c[...]))
    pair = choose(core, note_weights(msg_u, mols, 0), note_weights(msg_c, mols, 0))
    c[1] = couple(rows, back[...], twice(pair))


def right_body(states, rho_a, low, high, metric, proj_a, own, msg_r, proj_r, back_r, c):
    mols = rho_a.shape[0]
    rows = stack_two(low, high, states)
    proj_r[...] = dot(rows, metric[...]).astype(BF)
    back_r[...] = dot_nt(rows, metric[...]).astype(BF)
    c[0] = couple(proj_a[...], rows, own[...])
    c[1] = couple(proj_r[...], stack(rho_a, states), twice(note_weights(msg_r, mols, 0)))


def fields(states, core, y_a, msg_r, msg_u, msg_c):
    field = y_a.shape[1]
    f_a = stack(y_a, states)
    f_r, f_u, f_c = [stack(m[:, :field], states) for m in (msg_r, msg_u, msg_c)]
    return f_a, f_r, f_u, choose(core, f_u, f_c), choose(core, f_c, f_u)


def sums_of(core, c_aa, c_f, c_r, c_s, f_a, f_r, f_u, f_first, f_last):
    row_a = (dot(c_aa[...], f_a) + dot(c_f[0], f_first)) + (dot(c_r[0], f_r) + dot(c_s[0], f_last))
    row_r = dot(c_r[1], f_a) + dot(c_s[2], f_u)
    first, last = dot(c_f[1], f_a), dot(c_s[1], f_a)
    row_u = choose(core, first, last) + dot(c_s[3], f_r)
    return row_a, row_r, row_u, choose(core, last, first)


def corner_body(
    states,
    core,
    first_low,
    first_high,
    near_low,
    near_high,
    shift_low,
    shift_high,
    proj_a,
    back_a,
    proj_r,
    back_r,
    own_u,
    own_c,
    msg_r,
    msg_u,
    msg_c,
    y_a,
    e_a,
    c_aa,
    c_f,
    c_r,
    c,
    to_a,
    to_r,
    to_uc,
    sums,
    rows,
):
    mols, field = y_a.shape
    width = first_low.shape[1] * 2 // states
    halves = ((first_low, near_low, shift_low), (first_high, near_high, shift_high))
    for a in range(states):
        first, near, shifted = halves[a * 2 // states]
        b = a % (states // 2)
        lanes = slice(b * width, (b + 1) * width)
        place = slice(a * mols, (a + 1) * mols)
        rows[0, place] = first[:, lanes]
        rows[1, place] = choose(core, near[:, lanes], shifted[:, lanes])
    upper = rows.at[core[0, 0]]
    last = rows[1]
    c[0] = couple(proj_a[...], last, choose(core, own_c[...], own_u[...]))
    pair = choose(core, note_weights(msg_c, mols, 0), note_weights(msg_u, mols, 0))
    c[1] = couple(last, back_a[...], twice(pair))
    c[2] = couple(proj_r[...], upper[...], twice(note_weights(msg_r, mols, 1)))
    c[3] = couple(upper[...], back_r[...], twice(note_weights(msg_u, mols, 1)))
    f = fields(states, core, y_a, msg_r, msg_u, msg_c)
    row_a, row_r, row_u, row_c = sums_of(core, c_aa, c_f, c_r, c, *f)
    own_y = y_a[...].astype(F32)
    part_a = unstack(row_a, states) + spread(e_a[...], field // states) * own_y
    part_r, part_u, part_c = [unstack(row, states) for row in (row_r, row_u, row_c)]
    to_a[...], to_r[...], to_uc[0], to_uc[1] = part_a, part_r, part_u, part_c
    y_r, y_u, y_c = [m[:, :field].astype(F32) for m in (msg_r, msg_u, msg_c)]
    total = (part_a * own_y + part_r * y_r) + (part_u * y_u + part_c * y_c)
    sums[0:1] = jnp.sum(total, axis=0, keepdims=True)
    sums[1:2] = jnp.sum(own_y * own_y, axis=0, keepdims=True)


def over_states(row, width):
    states = row.shape[1] // width
    total = row[:, :width]
    for a in range(1, states):
        total = total + row[:, a * width : (a + 1) * width]
    return jnp.concatenate([total] * states, axis=1)


def residual(sigma, y, e, theta, width):
    return (sigma - theta * y) / jnp.maximum(jnp.abs(spread(e, width) - theta), 1.0)


def theta_body(states, part, rest, sigma, y_a, e_a, theta, short, resid, squares):
    width = sigma.shape[1] // states
    sums = part[...] + rest[...]
    rate = over_states(sums[0:1], width) / over_states(sums[1:2], width)
    theta[...] = rate
    short[...] = rate[:, :width]
    value = residual(sigma[...], y_a[...].astype(F32), e_a[...], rate, width)
    resid[...] = value
    squares[...] = jnp.sum(value * value, axis=0, keepdims=True)


def second_body(
    states,
    core,
    theta,
    resid,
    sig_r,
    sig_uc,
    msg_r,
    msg_u,
    msg_c,
    c_aa,
    c_f,
    c_r,
    c_s,
    to_a,
    to_r,
    to_uc,
):
    _, field = resid.shape
    width = field // states

    def other(sigma, msg):
        e = note_energies(msg, states)
        value = residual(sigma, msg[:, :field].astype(F32), e, theta[...], width)
        return stack(value, states).astype(BF)

    f_a = stack(resid[...], states).astype(BF)
    f_r = other(sig_r[...], msg_r)
    f_u = other(sig_uc[0], msg_u)
    f_c = other(sig_uc[1], msg_c)
    rows = sums_of(
        core, c_aa, c_f, c_r, c_s, f_a, f_r, f_u, choose(core, f_u, f_c), choose(core, f_c, f_u)
    )
    to_a[...], to_r[...], to_uc[0], to_uc[1] = [unstack(row, states) for row in rows]


def last_body(states, count, part, rest, resid, to_a, below, left, e_a, corr, sigma):
    width = resid.shape[1] // states
    scale = jnp.sqrt(over_states(part[...] + rest[...], width) / count + 1e-06)
    value = (resid[...] / scale).astype(BF)
    corr[...] = value
    raw = (to_a[...] + below[0]) + left[...]
    sigma[...] = raw / scale + spread(e_a[...], width) * value.astype(F32)


def shards(densities, trials, energies, metric, pair_local, pair_remote, pair_scale):
    mols = densities.shape[2]
    states = energies.shape[3]
    aux = metric.shape[0]
    field = trials.shape[3]
    pairs = pair_local.shape[2]
    width = mols * states
    nx, ny = lax.axis_size("gx"), lax.axis_size("gy")

    def spot(x, y):
        return (x % nx) * ny + y % ny

    def take(value, dx, dy, only=lambda x, y: True):
        table = [
            (spot(x + dx, y + dy), spot(x, y))
            for x in range(nx)
            for y in range(ny)
            if only(x, y)
        ]
        return lax.ppermute(value, AXES, table)

    def along_z(table):
        def partner(x, y):
            z = table[(y // 2 % 2) * 4 + x % 4]
            return x // 4 * 4 + z % 4, y // 4 * 4 + z // 4 * 2 + y % 2

        return partner

    def flip(fx, fy):
        return lambda x, y: (x ^ fx, y ^ fy)

    steps = [
        along_z((3, 6, 5, 0, 7, 2, 1, 4)),
        along_z((7, 2, 1, 4, 3, 6, 5, 0)),
        along_z((1, 0, 3, 2, 5, 4, 7, 6)),
        flip(0, 4),
        flip(0, 12),
        flip(4, 0),
        flip(12, 0),
        flip(0, 1),
    ]
    z_far, z_mid, z_near, x_near, x_far, y_near, y_far, chip = steps

    def butterfly(value, steps):
        for k, partner in enumerate(steps):
            table = [(spot(*partner(x, y)), spot(x, y)) for x in range(nx) for y in range(ny)]
            other = lax.ppermute(value, AXES, table)
            if k == len(steps) - 1:
                return value, other
            value = value + other

    rho_a, y_a, e_a = densities[0, 0], trials[0, 0], energies[0, 0]
    core = (lax.axis_index("gy") % 2).astype(jnp.int32).reshape(1, 1)
    table = [(spot(x + y % 2, y + 1), spot(x, y)) for x in range(nx) for y in range(ny)]
    half = rho_a.shape[1] // 2
    first_low = lax.ppermute(rho_a[:, :half], AXES, table)
    first_high = lax.ppermute(rho_a[:, half:], AXES, table)

    pair = shape(mols, 2 * mols)
    note = shape(mols, field + 6 * mols, dtype=BF)
    own_a, own_r, own_u, own_c, msg_r, msg_u, msg_c = call(
        functools.partial(weights_body, aux**-0.5),
        (pair, pair, pair, pair, note, note, note),
        9 * 2 * 3 * mols * 2 * mols * (pairs // 9),
        12 * pairs,
    )(pair_local[0], pair_remote[0], pair_scale[0], y_a, e_a)
    msg_r = take(msg_r, 1, 0)
    msg_u = take(msg_u, 0, 1)
    msg_c = take(msg_c, 1, 1)

    even, odd = (lambda x, y: y % 2 == 0), (lambda x, y: y % 2 == 1)
    right_low = take(rho_a[:, :half], 1, 0)
    right_high = take(rho_a[:, half:], 1, 0)
    shift_low = take(first_low, -1, 0, odd)
    shift_high = take(first_high, -1, 0, odd)
    near_low = take(right_low, 0, 1, even)
    near_high = take(right_high, 0, 1, even)

    block = 2 * width * width * aux
    proj = 2 * width * aux * aux
    size = width * aux * 2
    wide, square = shape(width, aux, dtype=BF), shape(width, width, dtype=BF)
    squares_of = lambda count: shape(count, width, width, dtype=BF)
    proj_a, back_a, c_aa = call(
        functools.partial(self_body, states), (wide, wide, square), 2 * proj + block, 5 * size
    )(rho_a, metric, own_a)
    c_f = call(functools.partial(first_body, states), squares_of(2), 2 * block, 4 * size, 1)(
        core, first_low, first_high, proj_a, back_a, own_u, own_c, msg_u, msg_c
    )
    proj_r, back_r, c_r = call(
        functools.partial(right_body, states),
        (wide, wide, squares_of(2)),
        2 * proj + 2 * block,
        8 * size,
    )(rho_a, right_low, right_high, metric, proj_a, own_r, msg_r)
    one, two = shape(mols, field), shape(2, mols, field)
    c_s, to_a, to_r, to_uc, sums = call(
        functools.partial(corner_body, states),
        (squares_of(4), one, one, two, shape(2, field)),
        4 * block,
        9 * size,
        1,
        [pltpu.VMEM((2, width, aux), BF)],
    )(
        core,
        first_low,
        first_high,
        near_low,
        near_high,
        shift_low,
        shift_high,
        proj_a,
        back_a,
        proj_r,
        back_r,
        own_u,
        own_c,
        msg_r,
        msg_u,
        msg_c,
        y_a,
        e_a,
        c_aa,
        c_f,
        c_r,
    )

    def home(to_r, to_uc):
        below = take(to_uc, 0, -1)
        left = take(to_r + below[1], -1, 0)
        return below, left

    sums = butterfly(sums, [z_far, chip, z_mid, z_near, x_near, x_far, y_near, y_far])
    below, left = home(to_r, to_uc)
    sigma = (to_a + below[0]) + left
    sig_r = take(sigma, 1, 0)
    sig_uc = take(jnp.stack([sigma, sig_r]), 0, 1)
    theta, short, resid, squares = call(
        functools.partial(theta_body, states),
        (shape(1, field), shape(1, field // states), one, shape(1, field)),
        20 * mols * field,
        12 * mols * field,
    )(*sums, sigma, y_a, e_a)
    to_a, to_r, to_uc = call(
        functools.partial(second_body, states),
        (one, one, two),
        9 * 2 * width * field * mols,
        9 * width * width * 2,
        1,
    )(core, theta, resid, sig_r, sig_uc, msg_r, msg_u, msg_c, c_aa, c_f, c_r, c_s)
    squares = butterfly(squares, [x_near, z_far, chip, z_mid, z_near, x_far, y_near, y_far])
    below, left = home(to_r, to_uc)
    corr, sigma2 = call(
        functools.partial(last_body, states, float(width * nx * ny)),
        (shape(mols, field, dtype=BF), one),
        20 * mols * field,
        16 * mols * field,
    )(*squares, resid, to_a, below, left, e_a)
    out = (1, 1, mols, field)
    return (
        sigma.reshape(out),
        corr.reshape(out),
        sigma2.reshape(out),
        short.reshape(field // states),
    )


def solution(mesh):
    return jax.shard_map(
        shards,
        mesh=mesh,
        in_specs=(
            P("gx", "gy", None, None),
            P("gx", "gy", None, None),
            P("gx", "gy", None, None),
            P(),
            P("gx", "gy", None),
            P("gx", "gy", None),
            P("gx", "gy", None),
        ),
        out_specs=(
            P("gx", "gy", None, None),
            P("gx", "gy", None, None),
            P("gx", "gy", None, None),
            P(),
        ),
        check_vma=False,
    )
```

```python
import functools

import jax
import jax.numpy as jnp
from jax import lax
from jax.experimental import pallas as pl
from jax.experimental.pallas import tpu as pltpu
from jax.sharding import PartitionSpec as P


BF = jnp.bfloat16
F32 = jnp.float32
AXES = ("gx", "gy")
SELF, TO_R, TO_U, TO_UR = 4, 7, 5, 8
R_TO_A, R_TO_U, U_TO_A, U_TO_R, UR_TO_A = 1, 2, 3, 6, 0


def vmem(count):
    return [pl.BlockSpec(memory_space=pltpu.VMEM)] * count


def call(body, outs, flops, moved, smem=0, scratch=()):
    return lambda *args: pl.pallas_call(
        body,
        out_shape=outs,
        in_specs=[pl.BlockSpec(memory_space=pltpu.SMEM)] * smem + vmem(len(args) - smem),
        out_specs=jax.tree.map(lambda _: pl.BlockSpec(memory_space=pltpu.VMEM), outs),
        scratch_shapes=scratch,
        compiler_params=pltpu.CompilerParams(vmem_limit_bytes=24 * 2**20),
        cost_estimate=pl.CostEstimate(flops=flops, bytes_accessed=moved, transcendentals=0),
    )(*args)


def shape(*dims, dtype=F32):
    return jax.ShapeDtypeStruct(dims, dtype)


def stack(ref, states):
    width = ref.shape[1] // states
    return jnp.concatenate([ref[:, a * width : (a + 1) * width] for a in range(states)], axis=0)


def unstack(value, states):
    mols = value.shape[0] // states
    return jnp.concatenate([value[a * mols : (a + 1) * mols] for a in range(states)], axis=1)


def dot_nt(a, b):
    return lax.dot_general(a, b, (((1,), (1,)), ((), ())), preferred_element_type=F32)


def dot(a, b):
    return jnp.dot(a, b, preferred_element_type=F32)


def twice(w):
    return jnp.concatenate([w, w], axis=1)


def couple(proj, rho, pair):
    dense = dot_nt(proj, rho)
    tiles = (dense.shape[0] // pair.shape[0], dense.shape[1] // pair.shape[1])
    return (dense * jnp.tile(pair, tiles)).astype(BF)


def spread(e, width):
    mols, states = e.shape
    lane = lax.broadcasted_iota(jnp.int32, (mols, states * width), 1) // width
    out = jnp.zeros((mols, states * width), F32)
    for a in range(states):
        out = jnp.where(lane == a, e[:, a : a + 1], out)
    return out


def weights_body(scale, loc, rem, sc, y, e, own_a, own_r, own_u, own_c, msg_r, msg_u, msg_c):
    mols = y.shape[0]
    cap = loc.shape[1] // 9
    mol = lax.broadcasted_iota(jnp.int32, (mols, cap), 0)

    def weight(o):
        part = slice(o * cap, (o + 1) * cap)
        left, right, factor = loc[:, part], rem[:, part], sc[:, part] * scale
        if o == 4:
            right = left + 1 + right
            right = jnp.where(right >= mols, right - mols, right)
        mine = jnp.where(mol == left, factor, 0.0)
        far = jnp.where(mol == right, 1.0, 0.0).astype(BF)
        three = dot_nt(
            jnp.concatenate(split(mine, 3), axis=0), jnp.concatenate([far, far], axis=0)
        )
        return three[:mols] + (three[mols : 2 * mols] + three[2 * mols :])

    for own, o in ((own_a, SELF), (own_r, TO_R), (own_u, TO_U), (own_c, TO_UR)):
        own[...] = weight(o)
    for msg, o, q in (
        (msg_r, R_TO_A, R_TO_U),
        (msg_u, U_TO_A, U_TO_R),
        (msg_c, UR_TO_A, None),
    ):
        first = weight(o)
        if q is not None:
            lane = lax.broadcasted_iota(jnp.int32, first.shape, 1)
            first = jnp.where(lane < mols, first, weight(q))
        energies = split(e[...], 3)
        used = 3 * e.shape[1]
        parts = [y[...], *split(first, 2), *energies, jnp.zeros((mols, 2 * mols - used), BF)]
        msg[...] = jnp.concatenate(parts, axis=1)


def choose(core, low, high):
    return jnp.where(core[0, 0] == 1, high, low)


def self_body(states, rho, metric, own, proj, back, c_aa):
    rows = stack(rho, states)
    proj[...] = dot(rows, metric[...]).astype(BF)
    back[...] = dot_nt(rows, metric[...]).astype(BF)
    c_aa[...] = couple(proj[...], rows, own[...])


def stack_two(low, high, states):
    return jnp.concatenate([stack(low, states // 2), stack(high, states // 2)], axis=0)


def cut_body(rho, low, high, sems):
    half = low.shape[1]
    copies = [
        pltpu.make_async_copy(rho.at[:, k * half : (k + 1) * half], out, sems.at[k])
        for k, out in enumerate((low, high))
    ]
    for copy in copies:
        copy.start()
    for copy in copies:
        copy.wait()


def note_weights(note, mols, k):
    base = note.shape[1] - 6 * mols + k * mols
    high, low = note[:, base : base + mols], note[:, base + 2 * mols : base + 3 * mols]
    return high.astype(F32) + low.astype(F32)


def note_energies(note, states):
    base = note.shape[1] - 2 * note.shape[0]
    parts = [note[:, base + k * states : base + (k + 1) * states].astype(F32) for k in range(3)]
    return parts[0] + (parts[1] + parts[2])


def split(value, count):
    parts = []
    for _ in range(count):
        parts.append(value.astype(BF))
        value = value - parts[-1].astype(F32)
    return parts


def first_body(states, core, low, high, proj, back, own_u, own_c, msg_u, msg_c, c):
    mols = low.shape[0]
    rows = stack_two(low, high, states)
    c[0] = couple(proj[...], rows, choose(core, own_u[...], own_c[...]))
    pair = choose(core, note_weights(msg_u, mols, 0), note_weights(msg_c, mols, 0))
    c[1] = couple(rows, back[...], twice(pair))


def right_body(states, rho_a, low, high, metric, proj_a, own, msg_r, proj_r, back_r, c):
    mols = rho_a.shape[0]
    rows = stack_two(low, high, states)
    proj_r[...] = dot(rows, metric[...]).astype(BF)
    back_r[...] = dot_nt(rows, metric[...]).astype(BF)
    c[0] = couple(proj_a[...], rows, own[...])
    c[1] = couple(proj_r[...], stack(rho_a, states), twice(note_weights(msg_r, mols, 0)))


def fields(states, core, y_a, msg_r, msg_u, msg_c):
    field = y_a.shape[1]
    f_a = stack(y_a, states)
    f_r, f_u, f_c = [stack(m[:, :field], states) for m in (msg_r, msg_u, msg_c)]
    return f_a, f_r, f_u, choose(core, f_u, f_c), choose(core, f_c, f_u)


def sums_of(core, c_aa, c_f, c_r, c_s, f_a, f_r, f_u, f_first, f_last):
    row_a = (dot(c_aa[...], f_a) + dot(c_f[0], f_first)) + (dot(c_r[0], f_r) + dot(c_s[0], f_last))
    row_r = dot(c_r[1], f_a) + dot(c_s[2], f_u)
    first, last = dot(c_f[1], f_a), dot(c_s[1], f_a)
    row_u = choose(core, first, last) + dot(c_s[3], f_r)
    return row_a, row_r, row_u, choose(core, last, first)


def corner_body(
    states,
    core,
    first_low,
    first_high,
    near_low,
    near_high,
    shift_low,
    shift_high,
    proj_a,
    back_a,
    proj_r,
    back_r,
    own_u,
    own_c,
    msg_r,
    msg_u,
    msg_c,
    y_a,
    e_a,
    c_aa,
    c_f,
    c_r,
    c,
    to_a,
    to_r,
    to_uc,
    sums,
    rows,
):
    mols, field = y_a.shape
    width = first_low.shape[1] * 2 // states
    halves = ((first_low, near_low, shift_low), (first_high, near_high, shift_high))
    for a in range(states):
        first, near, shifted = halves[a * 2 // states]
        b = a % (states // 2)
        lanes = slice(b * width, (b + 1) * width)
        place = slice(a * mols, (a + 1) * mols)
        rows[0, place] = first[:, lanes]
        rows[1, place] = choose(core, near[:, lanes], shifted[:, lanes])
    upper = rows.at[core[0, 0]]
    last = rows[1]
    c[0] = couple(proj_a[...], last, choose(core, own_c[...], own_u[...]))
    pair = choose(core, note_weights(msg_c, mols, 0), note_weights(msg_u, mols, 0))
    c[1] = couple(last, back_a[...], twice(pair))
    c[2] = couple(proj_r[...], upper[...], twice(note_weights(msg_r, mols, 1)))
    c[3] = couple(upper[...], back_r[...], twice(note_weights(msg_u, mols, 1)))
    f = fields(states, core, y_a, msg_r, msg_u, msg_c)
    row_a, row_r, row_u, row_c = sums_of(core, c_aa, c_f, c_r, c, *f)
    own_y = y_a[...].astype(F32)
    part_a = unstack(row_a, states) + spread(e_a[...], field // states) * own_y
    part_r, part_u, part_c = [unstack(row, states) for row in (row_r, row_u, row_c)]
    to_a[...], to_r[...], to_uc[0], to_uc[1] = part_a, part_r, part_u, part_c
    y_r, y_u, y_c = [m[:, :field].astype(F32) for m in (msg_r, msg_u, msg_c)]
    total = (part_a * own_y + part_r * y_r) + (part_u * y_u + part_c * y_c)
    sums[0:1] = jnp.sum(total, axis=0, keepdims=True)
    sums[1:2] = jnp.sum(own_y * own_y, axis=0, keepdims=True)


def over_states(row, width):
    states = row.shape[1] // width
    total = row[:, :width]
    for a in range(1, states):
        total = total + row[:, a * width : (a + 1) * width]
    return jnp.concatenate([total] * states, axis=1)


def residual(sigma, y, e, theta, width):
    return (sigma - theta * y) / jnp.maximum(jnp.abs(spread(e, width) - theta), 1.0)


def theta_body(states, part, rest, sigma, y_a, e_a, theta, short, resid, squares):
    width = sigma.shape[1] // states
    sums = part[...] + rest[...]
    rate = over_states(sums[0:1], width) / over_states(sums[1:2], width)
    theta[...] = rate
    short[...] = rate[:, :width]
    value = residual(sigma[...], y_a[...].astype(F32), e_a[...], rate, width)
    resid[...] = value
    squares[...] = jnp.sum(value * value, axis=0, keepdims=True)


def second_body(
    states,
    core,
    theta,
    resid,
    sig_r,
    sig_uc,
    msg_r,
    msg_u,
    msg_c,
    c_aa,
    c_f,
    c_r,
    c_s,
    to_a,
    to_r,
    to_uc,
):
    _, field = resid.shape
    width = field // states

    def other(sigma, msg):
        e = note_energies(msg, states)
        value = residual(sigma, msg[:, :field].astype(F32), e, theta[...], width)
        return stack(value, states).astype(BF)

    f_a = stack(resid[...], states).astype(BF)
    f_r = other(sig_r[...], msg_r)
    f_u = other(sig_uc[0], msg_u)
    f_c = other(sig_uc[1], msg_c)
    rows = sums_of(
        core, c_aa, c_f, c_r, c_s, f_a, f_r, f_u, choose(core, f_u, f_c), choose(core, f_c, f_u)
    )
    to_a[...], to_r[...], to_uc[0], to_uc[1] = [unstack(row, states) for row in rows]


def last_body(states, count, part, rest, resid, to_a, below, left, e_a, corr, sigma):
    width = resid.shape[1] // states
    scale = jnp.sqrt(over_states(part[...] + rest[...], width) / count + 1e-06)
    value = (resid[...] / scale).astype(BF)
    corr[...] = value
    raw = (to_a[...] + below[0]) + left[...]
    sigma[...] = raw / scale + spread(e_a[...], width) * value.astype(F32)


def shards(densities, trials, energies, metric, pair_local, pair_remote, pair_scale):
    mols = densities.shape[2]
    states = energies.shape[3]
    aux = metric.shape[0]
    field = trials.shape[3]
    pairs = pair_local.shape[2]
    width = mols * states
    nx, ny = lax.axis_size("gx"), lax.axis_size("gy")

    def spot(x, y):
        return (x % nx) * ny + y % ny

    def take(value, dx, dy, only=lambda x, y: True):
        table = [
            (spot(x + dx, y + dy), spot(x, y))
            for x in range(nx)
            for y in range(ny)
            if only(x, y)
        ]
        return lax.ppermute(value, AXES, table)

    def along_z(table):
        def partner(x, y):
            z = table[(y // 2 % 2) * 4 + x % 4]
            return x // 4 * 4 + z % 4, y // 4 * 4 + z // 4 * 2 + y % 2

        return partner

    def flip(fx, fy):
        return lambda x, y: (x ^ fx, y ^ fy)

    steps = [
        along_z((3, 6, 5, 0, 7, 2, 1, 4)),
        along_z((7, 2, 1, 4, 3, 6, 5, 0)),
        along_z((1, 0, 3, 2, 5, 4, 7, 6)),
        flip(0, 4),
        flip(0, 12),
        flip(4, 0),
        flip(12, 0),
        flip(0, 1),
    ]
    z_far, z_mid, z_near, x_near, x_far, y_near, y_far, chip = steps

    def butterfly(value, steps):
        for k, partner in enumerate(steps):
            table = [(spot(*partner(x, y)), spot(x, y)) for x in range(nx) for y in range(ny)]
            other = lax.ppermute(value, AXES, table)
            if k == len(steps) - 1:
                return value, other
            value = value + other

    rho_a, y_a, e_a = densities[0, 0], trials[0, 0], energies[0, 0]
    core = (lax.axis_index("gy") % 2).astype(jnp.int32).reshape(1, 1)
    piece = shape(mols, rho_a.shape[1] // 2, dtype=BF)
    own_low, own_high = pl.pallas_call(
        cut_body,
        out_shape=(piece, piece),
        in_specs=[pl.BlockSpec(memory_space=pltpu.HBM)],
        out_specs=(pl.BlockSpec(memory_space=pltpu.VMEM),) * 2,
        scratch_shapes=[pltpu.SemaphoreType.DMA((2,))],
        compiler_params=pltpu.CompilerParams(vmem_limit_bytes=4 * 2**20),
    )(rho_a)
    table = [(spot(x + y % 2, y + 1), spot(x, y)) for x in range(nx) for y in range(ny)]
    first_low = lax.ppermute(own_low, AXES, table)
    first_high = lax.ppermute(own_high, AXES, table)

    pair = shape(mols, 2 * mols)
    note = shape(mols, field + 6 * mols, dtype=BF)
    own_a, own_r, own_u, own_c, msg_r, msg_u, msg_c = call(
        functools.partial(weights_body, aux**-0.5),
        (pair, pair, pair, pair, note, note, note),
        9 * 2 * 3 * mols * 2 * mols * (pairs // 9),
        12 * pairs,
    )(pair_local[0], pair_remote[0], pair_scale[0], y_a, e_a)
    msg_r = take(msg_r, 1, 0)
    msg_u = take(msg_u, 0, 1)
    msg_c = take(msg_c, 1, 1)

    even, odd = (lambda x, y: y % 2 == 0), (lambda x, y: y % 2 == 1)
    right_low = take(own_low, 1, 0)
    right_high = take(own_high, 1, 0)
    shift_low = take(first_low, -1, 0, odd)
    shift_high = take(first_high, -1, 0, odd)
    near_low = take(right_low, 0, 1, even)
    near_high = take(right_high, 0, 1, even)

    block = 2 * width * width * aux
    proj = 2 * width * aux * aux
    size = width * aux * 2
    wide, square = shape(width, aux, dtype=BF), shape(width, width, dtype=BF)
    squares_of = lambda count: shape(count, width, width, dtype=BF)
    proj_a, back_a, c_aa = call(
        functools.partial(self_body, states), (wide, wide, square), 2 * proj + block, 5 * size
    )(rho_a, metric, own_a)
    c_f = call(functools.partial(first_body, states), squares_of(2), 2 * block, 4 * size, 1)(
        core, first_low, first_high, proj_a, back_a, own_u, own_c, msg_u, msg_c
    )
    proj_r, back_r, c_r = call(
        functools.partial(right_body, states),
        (wide, wide, squares_of(2)),
        2 * proj + 2 * block,
        8 * size,
    )(rho_a, right_low, right_high, metric, proj_a, own_r, msg_r)
    one, two = shape(mols, field), shape(2, mols, field)
    c_s, to_a, to_r, to_uc, sums = call(
        functools.partial(corner_body, states),
        (squares_of(4), one, one, two, shape(2, field)),
        4 * block,
        9 * size,
        1,
        [pltpu.VMEM((2, width, aux), BF)],
    )(
        core,
        first_low,
        first_high,
        near_low,
        near_high,
        shift_low,
        shift_high,
        proj_a,
        back_a,
        proj_r,
        back_r,
        own_u,
        own_c,
        msg_r,
        msg_u,
        msg_c,
        y_a,
        e_a,
        c_aa,
        c_f,
        c_r,
    )

    def home(to_r, to_uc):
        below = take(to_uc, 0, -1)
        left = take(to_r + below[1], -1, 0)
        return below, left

    sums = butterfly(sums, [z_far, chip, z_mid, z_near, x_near, x_far, y_near, y_far])
    below, left = home(to_r, to_uc)
    sigma = (to_a + below[0]) + left
    sig_r = take(sigma, 1, 0)
    sig_uc = take(jnp.stack([sigma, sig_r]), 0, 1)
    theta, short, resid, squares = call(
        functools.partial(theta_body, states),
        (shape(1, field), shape(1, field // states), one, shape(1, field)),
        20 * mols * field,
        12 * mols * field,
    )(*sums, sigma, y_a, e_a)
    to_a, to_r, to_uc = call(
        functools.partial(second_body, states),
        (one, one, two),
        9 * 2 * width * field * mols,
        9 * width * width * 2,
        1,
    )(core, theta, resid, sig_r, sig_uc, msg_r, msg_u, msg_c, c_aa, c_f, c_r, c_s)
    squares = butterfly(squares, [x_near, x_far, z_far, chip, z_mid, z_near, y_near, y_far])
    below, left = home(to_r, to_uc)
    corr, sigma2 = call(
        functools.partial(last_body, states, float(width * nx * ny)),
        (shape(mols, field, dtype=BF), one),
        20 * mols * field,
        16 * mols * field,
    )(*squares, resid, to_a, below, left, e_a)
    out = (1, 1, mols, field)
    return (
        sigma.reshape(out),
        corr.reshape(out),
        sigma2.reshape(out),
        short.reshape(field // states),
    )


def solution(mesh):
    return jax.shard_map(
        shards,
        mesh=mesh,
        in_specs=(
            P("gx", "gy", None, None),
            P("gx", "gy", None, None),
            P("gx", "gy", None, None),
            P(),
            P("gx", "gy", None),
            P("gx", "gy", None),
            P("gx", "gy", None),
        ),
        out_specs=(
            P("gx", "gy", None, None),
            P("gx", "gy", None, None),
            P("gx", "gy", None, None),
            P(),
        ),
        check_vma=False,
    )
```

```python
import functools

import jax
import jax.numpy as jnp
from jax import lax
from jax.experimental import pallas as pl
from jax.experimental.pallas import tpu as pltpu
from jax.sharding import PartitionSpec as P


BF = jnp.bfloat16
F32 = jnp.float32
AXES = ("gx", "gy")
SELF, TO_R, TO_U, TO_UR = 4, 7, 5, 8
R_TO_A, R_TO_U, U_TO_A, U_TO_R, UR_TO_A = 1, 2, 3, 6, 0


def vmem(count):
    return [pl.BlockSpec(memory_space=pltpu.VMEM)] * count


def call(body, outs, flops, moved, smem=0, scratch=()):
    return lambda *args: pl.pallas_call(
        body,
        out_shape=outs,
        in_specs=[pl.BlockSpec(memory_space=pltpu.SMEM)] * smem + vmem(len(args) - smem),
        out_specs=jax.tree.map(lambda _: pl.BlockSpec(memory_space=pltpu.VMEM), outs),
        scratch_shapes=scratch,
        compiler_params=pltpu.CompilerParams(vmem_limit_bytes=24 * 2**20),
        cost_estimate=pl.CostEstimate(flops=flops, bytes_accessed=moved, transcendentals=0),
    )(*args)


def shape(*dims, dtype=F32):
    return jax.ShapeDtypeStruct(dims, dtype)


def stack(ref, states):
    width = ref.shape[1] // states
    return jnp.concatenate([ref[:, a * width : (a + 1) * width] for a in range(states)], axis=0)


def unstack(value, states):
    mols = value.shape[0] // states
    return jnp.concatenate([value[a * mols : (a + 1) * mols] for a in range(states)], axis=1)


def dot_nt(a, b):
    return lax.dot_general(a, b, (((1,), (1,)), ((), ())), preferred_element_type=F32)


def dot(a, b):
    return jnp.dot(a, b, preferred_element_type=F32)


def twice(w):
    return jnp.concatenate([w, w], axis=1)


def couple(proj, rho, pair):
    dense = dot_nt(proj, rho)
    tiles = (dense.shape[0] // pair.shape[0], dense.shape[1] // pair.shape[1])
    return (dense * jnp.tile(pair, tiles)).astype(BF)


def spread(e, width):
    mols, states = e.shape
    lane = lax.broadcasted_iota(jnp.int32, (mols, states * width), 1) // width
    out = jnp.zeros((mols, states * width), F32)
    for a in range(states):
        out = jnp.where(lane == a, e[:, a : a + 1], out)
    return out


def weights_body(scale, loc, rem, sc, y, e, own_a, own_r, own_u, own_c, msg_r, msg_u, msg_c):
    mols = y.shape[0]
    cap = loc.shape[1] // 9
    mol = lax.broadcasted_iota(jnp.int32, (mols, cap), 0)

    def weight(o):
        part = slice(o * cap, (o + 1) * cap)
        left, right, factor = loc[:, part], rem[:, part], sc[:, part] * scale
        if o == 4:
            right = left + 1 + right
            right = jnp.where(right >= mols, right - mols, right)
        mine = jnp.where(mol == left, factor, 0.0)
        far = jnp.where(mol == right, 1.0, 0.0).astype(BF)
        three = dot_nt(
            jnp.concatenate(split(mine, 3), axis=0), jnp.concatenate([far, far], axis=0)
        )
        return three[:mols] + (three[mols : 2 * mols] + three[2 * mols :])

    for own, o in ((own_a, SELF), (own_r, TO_R), (own_u, TO_U), (own_c, TO_UR)):
        own[...] = weight(o)
    for msg, o, q in (
        (msg_r, R_TO_A, R_TO_U),
        (msg_u, U_TO_A, U_TO_R),
        (msg_c, UR_TO_A, None),
    ):
        first = weight(o)
        if q is not None:
            lane = lax.broadcasted_iota(jnp.int32, first.shape, 1)
            first = jnp.where(lane < mols, first, weight(q))
        energies = split(e[...], 3)
        used = 3 * e.shape[1]
        parts = [y[...], *split(first, 2), *energies, jnp.zeros((mols, 2 * mols - used), BF)]
        msg[...] = jnp.concatenate(parts, axis=1)


def choose(core, low, high):
    return jnp.where(core[0, 0] == 1, high, low)


def self_body(states, rho, metric, own, proj, back, c_aa):
    rows = stack(rho, states)
    proj[...] = dot(rows, metric[...]).astype(BF)
    back[...] = dot_nt(rows, metric[...]).astype(BF)
    c_aa[...] = couple(proj[...], rows, own[...])


def stack_two(low, high, states):
    width = low.shape[1] // states
    return jnp.concatenate(
        [half[:, a * width : (a + 1) * width] for a in range(states) for half in (low, high)],
        axis=0,
    )


def note_weights(note, mols, k):
    base = note.shape[1] - 6 * mols + k * mols
    high, low = note[:, base : base + mols], note[:, base + 2 * mols : base + 3 * mols]
    return high.astype(F32) + low.astype(F32)


def note_energies(note, states):
    base = note.shape[1] - 2 * note.shape[0]
    parts = [note[:, base + k * states : base + (k + 1) * states].astype(F32) for k in range(3)]
    return parts[0] + (parts[1] + parts[2])


def split(value, count):
    parts = []
    for _ in range(count):
        parts.append(value.astype(BF))
        value = value - parts[-1].astype(F32)
    return parts


def first_body(states, core, low, high, proj, back, own_u, own_c, msg_u, msg_c, c):
    mols = 2 * low.shape[0]
    rows = stack_two(low, high, states)
    c[0] = couple(proj[...], rows, choose(core, own_u[...], own_c[...]))
    pair = choose(core, note_weights(msg_u, mols, 0), note_weights(msg_c, mols, 0))
    c[1] = couple(rows, back[...], twice(pair))


def right_body(states, rho_a, low, high, metric, proj_a, own, msg_r, proj_r, back_r, c):
    mols = rho_a.shape[0]
    rows = stack_two(low, high, states)
    proj_r[...] = dot(rows, metric[...]).astype(BF)
    back_r[...] = dot_nt(rows, metric[...]).astype(BF)
    c[0] = couple(proj_a[...], rows, own[...])
    c[1] = couple(proj_r[...], stack(rho_a, states), twice(note_weights(msg_r, mols, 0)))


def fields(states, core, y_a, msg_r, msg_u, msg_c):
    field = y_a.shape[1]
    f_a = stack(y_a, states)
    f_r, f_u, f_c = [stack(m[:, :field], states) for m in (msg_r, msg_u, msg_c)]
    return f_a, f_r, f_u, choose(core, f_u, f_c), choose(core, f_c, f_u)


def sums_of(core, c_aa, c_f, c_r, c_s, f_a, f_r, f_u, f_first, f_last):
    row_a = (dot(c_aa[...], f_a) + dot(c_f[0], f_first)) + (dot(c_r[0], f_r) + dot(c_s[0], f_last))
    row_r = dot(c_r[1], f_a) + dot(c_s[2], f_u)
    first, last = dot(c_f[1], f_a), dot(c_s[1], f_a)
    row_u = choose(core, first, last) + dot(c_s[3], f_r)
    return row_a, row_r, row_u, choose(core, last, first)


def corner_body(
    states,
    core,
    first_low,
    first_high,
    near_low,
    near_high,
    shift_low,
    shift_high,
    proj_a,
    back_a,
    proj_r,
    back_r,
    own_u,
    own_c,
    msg_r,
    msg_u,
    msg_c,
    y_a,
    e_a,
    c_aa,
    c_f,
    c_r,
    c,
    to_a,
    to_r,
    to_uc,
    sums,
    rows,
):
    mols, field = y_a.shape
    width = first_low.shape[1] // states
    halves = ((first_low, near_low, shift_low), (first_high, near_high, shift_high))
    for a in range(states):
        for k, (first, near, shifted) in enumerate(halves):
            lanes = slice(a * width, (a + 1) * width)
            start = a * mols + k * mols // 2
            place = slice(start, start + mols // 2)
            rows[0, place] = first[:, lanes]
            rows[1, place] = choose(core, near[:, lanes], shifted[:, lanes])
    upper = rows.at[core[0, 0]]
    last = rows[1]
    c[0] = couple(proj_a[...], last, choose(core, own_c[...], own_u[...]))
    pair = choose(core, note_weights(msg_c, mols, 0), note_weights(msg_u, mols, 0))
    c[1] = couple(last, back_a[...], twice(pair))
    c[2] = couple(proj_r[...], upper[...], twice(note_weights(msg_r, mols, 1)))
    c[3] = couple(upper[...], back_r[...], twice(note_weights(msg_u, mols, 1)))
    f = fields(states, core, y_a, msg_r, msg_u, msg_c)
    row_a, row_r, row_u, row_c = sums_of(core, c_aa, c_f, c_r, c, *f)
    own_y = y_a[...].astype(F32)
    part_a = unstack(row_a, states) + spread(e_a[...], field // states) * own_y
    part_r, part_u, part_c = [unstack(row, states) for row in (row_r, row_u, row_c)]
    to_a[...], to_r[...], to_uc[0], to_uc[1] = part_a, part_r, part_u, part_c
    y_r, y_u, y_c = [m[:, :field].astype(F32) for m in (msg_r, msg_u, msg_c)]
    total = (part_a * own_y + part_r * y_r) + (part_u * y_u + part_c * y_c)
    sums[0:1] = jnp.sum(total, axis=0, keepdims=True)
    sums[1:2] = jnp.sum(own_y * own_y, axis=0, keepdims=True)


def over_states(row, width):
    states = row.shape[1] // width
    total = row[:, :width]
    for a in range(1, states):
        total = total + row[:, a * width : (a + 1) * width]
    return jnp.concatenate([total] * states, axis=1)


def residual(sigma, y, e, theta, width):
    return (sigma - theta * y) / jnp.maximum(jnp.abs(spread(e, width) - theta), 1.0)


def theta_body(states, part, rest, sigma, y_a, e_a, theta, short, resid, squares):
    width = sigma.shape[1] // states
    sums = part[...] + rest[...]
    rate = over_states(sums[0:1], width) / over_states(sums[1:2], width)
    theta[...] = rate
    short[...] = rate[:, :width]
    value = residual(sigma[...], y_a[...].astype(F32), e_a[...], rate, width)
    resid[...] = value
    squares[...] = jnp.sum(value * value, axis=0, keepdims=True)


def second_body(
    states,
    core,
    theta,
    resid,
    sig_r,
    sig_uc,
    msg_r,
    msg_u,
    msg_c,
    c_aa,
    c_f,
    c_r,
    c_s,
    to_a,
    to_r,
    to_uc,
):
    _, field = resid.shape
    width = field // states

    def other(sigma, msg):
        e = note_energies(msg, states)
        value = residual(sigma, msg[:, :field].astype(F32), e, theta[...], width)
        return stack(value, states).astype(BF)

    f_a = stack(resid[...], states).astype(BF)
    f_r = other(sig_r[...], msg_r)
    f_u = other(sig_uc[0], msg_u)
    f_c = other(sig_uc[1], msg_c)
    rows = sums_of(
        core, c_aa, c_f, c_r, c_s, f_a, f_r, f_u, choose(core, f_u, f_c), choose(core, f_c, f_u)
    )
    to_a[...], to_r[...], to_uc[0], to_uc[1] = [unstack(row, states) for row in rows]


def last_body(states, count, part, rest, resid, to_a, below, left, e_a, corr, sigma):
    width = resid.shape[1] // states
    scale = jnp.sqrt(over_states(part[...] + rest[...], width) / count + 1e-06)
    value = (resid[...] / scale).astype(BF)
    corr[...] = value
    raw = (to_a[...] + below[0]) + left[...]
    sigma[...] = raw / scale + spread(e_a[...], width) * value.astype(F32)


def shards(densities, trials, energies, metric, pair_local, pair_remote, pair_scale):
    mols = densities.shape[2]
    states = energies.shape[3]
    aux = metric.shape[0]
    field = trials.shape[3]
    pairs = pair_local.shape[2]
    width = mols * states
    nx, ny = lax.axis_size("gx"), lax.axis_size("gy")

    def spot(x, y):
        return (x % nx) * ny + y % ny

    def take(value, dx, dy, only=lambda x, y: True):
        table = [
            (spot(x + dx, y + dy), spot(x, y))
            for x in range(nx)
            for y in range(ny)
            if only(x, y)
        ]
        return lax.ppermute(value, AXES, table)

    def along_z(table):
        def partner(x, y):
            z = table[(y // 2 % 2) * 4 + x % 4]
            return x // 4 * 4 + z % 4, y // 4 * 4 + z // 4 * 2 + y % 2

        return partner

    def flip(fx, fy):
        return lambda x, y: (x ^ fx, y ^ fy)

    steps = [
        along_z((3, 6, 5, 0, 7, 2, 1, 4)),
        along_z((7, 2, 1, 4, 3, 6, 5, 0)),
        along_z((1, 0, 3, 2, 5, 4, 7, 6)),
        flip(0, 4),
        flip(0, 12),
        flip(4, 0),
        flip(12, 0),
        flip(0, 1),
    ]
    z_far, z_mid, z_near, x_near, x_far, y_near, y_far, chip = steps

    def butterfly(value, steps):
        for k, partner in enumerate(steps):
            table = [(spot(*partner(x, y)), spot(x, y)) for x in range(nx) for y in range(ny)]
            other = lax.ppermute(value, AXES, table)
            if k == len(steps) - 1:
                return value, other
            value = value + other

    rho_a, y_a, e_a = densities[0, 0], trials[0, 0], energies[0, 0]
    core = (lax.axis_index("gy") % 2).astype(jnp.int32).reshape(1, 1)
    own_low, own_high = rho_a[: mols // 2], rho_a[mols // 2 :]
    table = [(spot(x + y % 2, y + 1), spot(x, y)) for x in range(nx) for y in range(ny)]
    first_low = lax.ppermute(own_low, AXES, table)
    first_high = lax.ppermute(own_high, AXES, table)

    pair = shape(mols, 2 * mols)
    note = shape(mols, field + 6 * mols, dtype=BF)
    own_a, own_r, own_u, own_c, msg_r, msg_u, msg_c = call(
        functools.partial(weights_body, aux**-0.5),
        (pair, pair, pair, pair, note, note, note),
        9 * 2 * 3 * mols * 2 * mols * (pairs // 9),
        12 * pairs,
    )(pair_local[0], pair_remote[0], pair_scale[0], y_a, e_a)
    msg_r = take(msg_r, 1, 0)
    msg_u = take(msg_u, 0, 1)
    msg_c = take(msg_c, 1, 1)

    even, odd = (lambda x, y: y % 2 == 0), (lambda x, y: y % 2 == 1)
    right_low = take(own_low, 1, 0)
    right_high = take(own_high, 1, 0)
    shift_low = take(first_low, -1, 0, odd)
    shift_high = take(first_high, -1, 0, odd)
    near_low = take(right_low, 0, 1, even)
    near_high = take(right_high, 0, 1, even)

    block = 2 * width * width * aux
    proj = 2 * width * aux * aux
    size = width * aux * 2
    wide, square = shape(width, aux, dtype=BF), shape(width, width, dtype=BF)
    squares_of = lambda count: shape(count, width, width, dtype=BF)
    proj_a, back_a, c_aa = call(
        functools.partial(self_body, states), (wide, wide, square), 2 * proj + block, 5 * size
    )(rho_a, metric, own_a)
    c_f = call(functools.partial(first_body, states), squares_of(2), 2 * block, 4 * size, 1)(
        core, first_low, first_high, proj_a, back_a, own_u, own_c, msg_u, msg_c
    )
    proj_r, back_r, c_r = call(
        functools.partial(right_body, states),
        (wide, wide, squares_of(2)),
        2 * proj + 2 * block,
        8 * size,
    )(rho_a, right_low, right_high, metric, proj_a, own_r, msg_r)
    one, two = shape(mols, field), shape(2, mols, field)
    c_s, to_a, to_r, to_uc, sums = call(
        functools.partial(corner_body, states),
        (squares_of(4), one, one, two, shape(2, field)),
        4 * block,
        9 * size,
        1,
        [pltpu.VMEM((2, width, aux), BF)],
    )(
        core,
        first_low,
        first_high,
        near_low,
        near_high,
        shift_low,
        shift_high,
        proj_a,
        back_a,
        proj_r,
        back_r,
        own_u,
        own_c,
        msg_r,
        msg_u,
        msg_c,
        y_a,
        e_a,
        c_aa,
        c_f,
        c_r,
    )

    def home(to_r, to_uc):
        below = take(to_uc, 0, -1)
        left = take(to_r + below[1], -1, 0)
        return below, left

    sums = butterfly(sums, [z_far, chip, z_mid, z_near, x_near, x_far, y_near, y_far])
    below, left = home(to_r, to_uc)
    sigma = (to_a + below[0]) + left
    sig_r = take(sigma, 1, 0)
    sig_uc = take(jnp.stack([sigma, sig_r]), 0, 1)
    theta, short, resid, squares = call(
        functools.partial(theta_body, states),
        (shape(1, field), shape(1, field // states), one, shape(1, field)),
        20 * mols * field,
        12 * mols * field,
    )(*sums, sigma, y_a, e_a)
    to_a, to_r, to_uc = call(
        functools.partial(second_body, states),
        (one, one, two),
        9 * 2 * width * field * mols,
        9 * width * width * 2,
        1,
    )(core, theta, resid, sig_r, sig_uc, msg_r, msg_u, msg_c, c_aa, c_f, c_r, c_s)
    squares = butterfly(squares, [x_near, x_far, z_far, chip, z_mid, z_near, y_near, y_far])
    below, left = home(to_r, to_uc)
    corr, sigma2 = call(
        functools.partial(last_body, states, float(width * nx * ny)),
        (shape(mols, field, dtype=BF), one),
        20 * mols * field,
        16 * mols * field,
    )(*squares, resid, to_a, below, left, e_a)
    out = (1, 1, mols, field)
    return (
        sigma.reshape(out),
        corr.reshape(out),
        sigma2.reshape(out),
        short.reshape(field // states),
    )


def solution(mesh):
    return jax.shard_map(
        shards,
        mesh=mesh,
        in_specs=(
            P("gx", "gy", None, None),
            P("gx", "gy", None, None),
            P("gx", "gy", None, None),
            P(),
            P("gx", "gy", None),
            P("gx", "gy", None),
            P("gx", "gy", None),
        ),
        out_specs=(
            P("gx", "gy", None, None),
            P("gx", "gy", None, None),
            P("gx", "gy", None, None),
            P(),
        ),
        check_vma=False,
    )
```
